32 devices in a mesh: pair: 8 (over z, y), aux: 4 (over x, core).
Axes of the slice: x: 2, y: 2, z: 4, core: 2. Of those that a mesh axis runs over, the one named last changes fastest.
Arguments:
- amplitudes: float32 [896, 8, 896], P('aux', 'pair'), may hold values from -6 to 6
- fitting: float32 [4, 896, 896], P('aux', 'pair'), may hold values from -0.09375 to 0.09375
Outputs:
- ladder: float32 [896, 8, 896], P('aux', 'pair')
The draws below stay inside these ranges and needn't reach their ends.
All inputs are finite; a program needn't handle non-finite values.
Results may differ from the reference program's by a relative error of at most 0.0001.
Values sent between devices are 32-bit elements; how exact they have to be, the bound alone decides.
A program may use at most 64 MiB of HBM per device.

```python
import jax
import jax.numpy as jnp
from jax import lax

V = 896
NPAIRS = 8
NFIT = 4


def level_of(own_key, extent, split, least, largest):
    gain, own = 1.0, jax.random.fold_in(own_key, 6)
    for position, parts in split:
        draws = jnp.exp(jax.random.uniform(jax.random.fold_in(own, position), (parts,), jnp.float32, least / len(split), largest / len(split)))
        gain = gain * jnp.repeat(draws, extent[position] // parts).reshape([-1 if axis == position else 1 for axis in range(len(extent))])
    return gain


def gaussian(stream_key, extent, width, reach, pieces=(), dtype=jnp.bfloat16):
    entries = width * jax.random.normal(stream_key, extent, jnp.float32)
    if pieces:
        entries = entries * level_of(stream_key, extent, pieces, -0.22, 0.18)
    return jnp.clip(entries, -reach, reach).astype(dtype)


def setup_inputs(seed: int = 0) -> dict:
    splits = jax.random.split(jax.random.key(seed), 3)
    amplitudes = gaussian(splits[0], (V, NPAIRS, V), 1.0, 6.0, ((0, 4), (1, 8)), jnp.float32)
    fitting = gaussian(splits[1], (NFIT, V, V), (V * 4) ** -0.5, 0.09375, ((0, 4), (1, 8)), jnp.float32)
    return dict(amplitudes=amplitudes, fitting=fitting)


def reference(amplitudes, fitting):
    flat = amplitudes.reshape(V * NPAIRS, V)

    def step(total, matrix):
        half = jnp.dot(flat, matrix.T, precision=lax.Precision.HIGHEST, preferred_element_type=jnp.float32)
        half = half.reshape(V, NPAIRS * V)
        return total + jnp.dot(matrix, half, precision=lax.Precision.HIGHEST, preferred_element_type=jnp.float32), None

    total, _ = lax.scan(step, jnp.zeros((V, NPAIRS * V), jnp.float32), fitting)
    return total.reshape(V, NPAIRS, V)
```

```python
import functools

import jax
import jax.numpy as jnp
from jax import lax
from jax.experimental import pallas as pl
from jax.experimental.pallas import tpu as pltpu
from jax.sharding import PartitionSpec as P

MESH = pl.DeviceIdType.MESH
CUTS, PARTS = 4, 8
F32, BF16 = jnp.float32, jnp.bfloat16
NT = (((1,), (1,)), ((), ()))


def ring_order(n):
    depth = 4 if n % 4 == 0 and n > 4 else 2
    width = n // depth
    if n % 2 or width < 2:
        return list(range(n))
    walk = []
    for z in range(depth):
        ys = range(1, width) if z % 2 == 0 else range(width - 1, 0, -1)
        walk += [z * width + y for y in ys]
    return walk + [z * width for z in range(depth - 1, -1, -1)]


def lookup(table, key):
    return sum(jnp.where(key == k, v, 0) for k, v in enumerate(table))


def split(v):
    high = v.astype(BF16).astype(F32)
    return high, v - high


def kernel(
    n, chips, parts, cuts,
    t_in, b_in, out,
    t_all, t_high, t_low, b_all, b_high, b_low, g_high, g_low,
    outbox, inbox, mine, final,
    local_sem, out_sem, right_send, right_recv, left_send, left_recv, bm_send, bm_recv,
    tx_send, tx_recv, tm_send, tm_recv, px_send, px_recv,
):
    rows_b, width = b_in.shape
    lanes = t_in.shape[1]
    tiles = width // lanes
    rows_t = t_in.shape[0] // tiles
    piece = rows_t // parts
    q = rows_t // rows_b
    reach = n // 2
    order = ring_order(n)
    where = [order.index(k) for k in range(n)]
    pair, aux = lax.axis_index("pair"), lax.axis_index("aux")
    chip, core = aux // 2, aux % 2
    mate = chip * 2 + (1 - core)
    spot = lookup(where, pair)

    def at(step):
        return lookup(order, lax.rem(spot + step + n, n))

    right, left = at(1), at(-1)

    def chip_at(step):
        return lax.rem(chip + step + chips, chips)

    barrier = pltpu.get_barrier_semaphore()
    greet = [(right, aux), (left, aux), (pair, mate)]
    greet += [(pair, chip_at(e) * 2 + core) for e in range(1, chips)]
    for who in greet:
        pl.semaphore_signal(barrier, inc=1, device_id=who, device_id_type=MESH)
    pl.semaphore_wait(barrier, len(greet))

    edges = [rows_b // 8 * k // cuts * 8 for k in range(cuts)] + [rows_b]
    bounds = [(a, b - a) for a, b in zip(edges, edges[1:])]

    def b_rows(block, h):
        start, size = bounds[h]
        return pl.ds(pl.multiple_of(block * rows_b + start, 8), size)

    def t_rows(owner, s):
        start = (owner * rows_t + s * piece) * tiles
        return pl.ds(pl.multiple_of(start, 8), piece * tiles)

    def t_own(s):
        return pl.ds(s * piece * tiles, piece * tiles)

    def hop(d, h, to_right):
        block = at(1 - d if to_right else d - 1)
        rows = b_rows(block, h)
        start, size = bounds[h]
        src = b_in.at[pl.ds(start, size)] if d == 1 else b_all.at[core, rows]
        send, recv = (right_send, right_recv) if to_right else (left_send, left_recv)
        return pltpu.make_async_remote_copy(
            src_ref=src,
            dst_ref=b_all.at[core, rows],
            send_sem=send.at[d - 1, h],
            recv_sem=recv.at[d - 1, h],
            device_id=(right if to_right else left, aux),
            device_id_type=MESH,
        )

    def arrive(d, h, from_left):
        rows = b_rows(at(-d if from_left else d), h)
        send, recv = (right_send, right_recv) if from_left else (left_send, left_recv)
        pltpu.make_async_remote_copy(
            src_ref=b_all.at[core, rows],
            dst_ref=b_all.at[core, rows],
            send_sem=send.at[d - 1, h],
            recv_sem=recv.at[d - 1, h],
            device_id=(left if from_left else right, aux),
            device_id_type=MESH,
        ).wait_recv()

    def carried(d, h, to_right):
        return d < reach or (h < cuts // 2) == to_right

    def b_mate(d, h, from_left, level):
        rows = b_rows(at(-d if from_left else d), h)
        start, size = bounds[h]
        side = 0 if from_left else 1
        return pltpu.make_async_remote_copy(
            src_ref=b_in.at[pl.ds(start, size)] if d == 0 else b_all.at[level, rows],
            dst_ref=b_all.at[level, rows],
            send_sem=bm_send.at[d, side, h],
            recv_sem=bm_recv.at[d, side, h],
            device_id=(pair, mate),
            device_id_type=MESH,
        )

    def t_cross(e, s):
        return pltpu.make_async_remote_copy(
            src_ref=t_in.at[t_own(s)],
            dst_ref=t_all.at[t_rows(aux, s)],
            send_sem=tx_send.at[e - 1, s],
            recv_sem=tx_recv.at[e - 1, s],
            device_id=(pair, chip_at(e) * 2 + core),
            device_id_type=MESH,
        )

    def t_mate(e, s):
        rows = t_rows(chip_at(-e) * 2 + core, s)
        return pltpu.make_async_remote_copy(
            src_ref=t_in.at[t_own(s)] if e == 0 else t_all.at[rows],
            dst_ref=t_all.at[rows],
            send_sem=tm_send.at[e, s],
            recv_sem=tm_recv.at[e, s],
            device_id=(pair, mate),
            device_id_type=MESH,
        )

    def t_landed(owner, s, send, recv):
        rows = t_rows(owner, s)
        pltpu.make_async_remote_copy(
            src_ref=t_all.at[rows], dst_ref=t_all.at[rows], send_sem=send, recv_sem=recv,
            device_id=(pair, mate), device_id_type=MESH,
        ).wait_recv()

    started = []

    def go(copy):
        copy.start()
        started.append(copy)

    for s in range(parts):
        for e in range(1, chips):
            go(t_cross(e, s))
        if s == 0:
            for h in range(cuts):
                for to_right in (True, False):
                    if carried(1, h, to_right):
                        go(hop(1, h, to_right))
    own_b = pltpu.make_async_copy(
        b_in, b_all.at[core, pl.ds(pl.multiple_of(pair * rows_b, 8), rows_b)], local_sem.at[0]
    )
    own_t = pltpu.make_async_copy(
        t_in, t_all.at[pl.ds(pl.multiple_of(aux * rows_t * tiles, 8), rows_t * tiles)], local_sem.at[1]
    )
    own_t.start()
    own_b.start()
    for s in range(parts):
        go(t_mate(0, s))
    for h in range(cuts):
        go(b_mate(0, h, True, core))

    aligned = piece % 16 == 0

    def t_split(start, size):
        rows = pl.ds(pl.multiple_of(start, 16), size)
        for k in range(tiles):
            high, low = split(t_all[pl.ds(start * tiles + k, size, stride=tiles), :])
            t_high[rows, k * lanes:(k + 1) * lanes] = high.astype(BF16)
            t_low[rows, k * lanes:(k + 1) * lanes] = low.astype(BF16)

    def t_part(owner, s):
        if aligned:
            t_split(owner * rows_t + s * piece, piece)

    def t_over(e, s):
        owner = chip_at(-e) * 2 + (1 - core)
        t_landed(owner, s, tm_send.at[e, s], tm_recv.at[e, s])
        t_part(owner, s)

    def relay(d):
        for h in range(cuts):
            for from_left in (True, False):
                if carried(d, h, from_left):
                    arrive(d, h, from_left)
                    if d < reach and carried(d + 1, h, from_left):
                        go(hop(d + 1, h, from_left))
                    go(b_mate(d, h, from_left, core))

    def b_over(d):
        for h in range(cuts):
            for from_left in (True, False):
                if carried(d, h, from_left) and (d > 0 or from_left):
                    b_mate(d, h, from_left, 1 - core).wait_recv()

    def t_step(s):
        for e in range(1, chips):
            owner = chip_at(-e) * 2 + core
            t_landed(owner, s, tx_send.at[e - 1, s], tx_recv.at[e - 1, s])
            go(t_mate(e, s))
            t_part(owner, s)
        if s:
            for e in range(1, chips):
                t_over(e, s - 1)

    own_t.wait()
    if aligned:
        @pl.loop(0, parts)
        def _(s):
            t_part(aux, s)

        for s in range(parts):
            t_over(0, s)
    else:
        for s in range(parts):
            t_over(0, s)
    own_b.wait()
    b_over(0)

    early = max(1, reach - 2)
    for d in range(1, early + 1):
        for s in range(parts * (d - 1) // early, parts * d // early):
            if s == parts * d // early - 1:
                relay(d)
            t_step(s)
    for e in range(1, chips):
        t_over(e, parts - 1)
    for d in range(1, early + 1):
        b_over(d)
    if not aligned:
        @pl.loop(0, width // 128)
        def _(i):
            t_split(i * 128, 128)

    spans = [[min(abs(where[k] - where[p]), n - abs(where[k] - where[p])) for p in range(n)] for k in range(n)]
    ready = [lookup([max(early, v) for v in spans[k]], pair) for k in range(n)]
    tile_ready = []
    for j in range(tiles):
        last = ready[j * lanes // rows_b]
        for k in range(j * lanes // rows_b + 1, (j * lanes + lanes - 1) // rows_b + 1):
            last = jnp.maximum(last, ready[k])
        tile_ready.append(last)

    def first_block(slot):
        return (chip_at(slot // q) * 2 + core) * q + lax.rem(slot, q)

    def g_block(slot, level):
        block = first_block(slot)
        high, low = split(b_all[level, pl.ds(pl.multiple_of(block * rows_b, 8), rows_b), :])
        both = jnp.concatenate([high, low], axis=0).astype(BF16)
        main = jnp.dot(both, t_high[...], preferred_element_type=F32)
        rest = jnp.dot(high.astype(BF16), t_low[...], preferred_element_type=F32)
        high, low = split(main[:rows_b] + (main[rows_b:] + rest))
        g_high[level, slot] = high.astype(BF16)
        g_low[level, slot] = low.astype(BF16)

    def unit(slot, j):
        total = None
        for level in range(2):
            high, low = g_high[level, slot], g_low[level, slot]
            if rows_b % 16 == 0:
                both = jnp.concatenate([high, low], axis=0)
                main = lax.dot_general(both, b_high[level, j], NT, preferred_element_type=F32)
                main = main[:rows_b] + main[rows_b:]
            else:
                main = lax.dot_general(high, b_high[level, j], NT, preferred_element_type=F32)
                main = main + lax.dot_general(low, b_high[level, j], NT, preferred_element_type=F32)
            main = main + lax.dot_general(high, b_low[level, j], NT, preferred_element_type=F32)
            total = main if total is None else total + main
        return total

    def p_cross(e, i, j):
        return pltpu.make_async_remote_copy(
            src_ref=outbox.at[e - 1, i, j], dst_ref=inbox.at[e - 1, i, j],
            send_sem=px_send.at[e - 1, i, j], recv_sem=px_recv.at[e - 1, i, j],
            device_id=(pair, chip_at(e) * 2 + core), device_id_type=MESH,
        )

    def g_ready(first, last, event):
        @pl.loop(first * 2, last * 2)
        def _(i):
            slot, level = i // 2, lax.rem(i, 2)

            @pl.when(lookup(ready, first_block(slot)) == event)
            def _():
                g_block(slot, level)

    def units(event):
        @pl.loop(0, (chips - 1) * q * tiles)
        def _(u):
            slot, j = u // tiles + q, lax.rem(u, tiles)
            e, i = slot // q, lax.rem(slot, q)
            due = jnp.maximum(lookup(ready, first_block(slot)), lookup(tile_ready, j))

            @pl.when(due == event)
            def _():
                outbox[e - 1, i, j] = unit(slot, j)
                p_cross(e, i, j).start()

    def tile_split(event):
        @pl.loop(0, tiles * 2)
        def _(i):
            j, level = i // 2, lax.rem(i, 2)

            @pl.when(lookup(tile_ready, j) == event)
            def _():
                high, low = split(b_all[level, pl.ds(pl.multiple_of(j * lanes, lanes), lanes), :])
                b_high[level, j] = high.astype(BF16)
                b_low[level, j] = low.astype(BF16)

    for event in range(early, reach + 1):
        if event > early:
            relay(event)
            b_over(event)
        g_ready(q, chips * q, event)
        tile_split(event)
        units(event)
        g_ready(0, q, event)

    @pl.loop(0, q * tiles)
    def _(u):
        i, j = u // tiles, lax.rem(u, tiles)
        mine[i, j] = unit(i, j)

    for event in range(early, reach + 1):
        @pl.loop(0, q * tiles)
        def _(u):
            i, j = u // tiles, lax.rem(u, tiles)
            due = jnp.maximum(lookup(ready, first_block(i)), lookup(tile_ready, j))

            @pl.when(due == event)
            def _():
                total = mine[i, j]
                for e in range(1, chips):
                    p_cross(e, i, j).wait_recv()
                    total = total + inbox[e - 1, i, j]
                final[pl.ds(i * (rows_b * tiles) + j, rows_b, stride=tiles), :] = total

    done = pltpu.make_async_copy(final, out, out_sem.at[0])
    done.start()
    for copy in started:
        copy.wait_send()
    for e in range(1, chips):
        for i in range(q):
            for j in range(tiles):
                p_cross(e, i, j).wait_send()
    done.wait()


def per_device(n, n_aux, amplitudes, fitting):
    rows_t, pair_dev, width = amplitudes.shape
    count_fit, rows_b, _ = fitting.shape
    assert pair_dev == 1 and count_fit == 1 and rows_t % rows_b == 0
    chips = n_aux // 2
    parts = max([p for p in range(1, PARTS + 1) if rows_t % (16 * p) == 0], default=1)
    cuts = CUTS
    reach = n // 2
    lanes = 128
    tiles = width // lanes
    q = rows_t // rows_b
    dma = pltpu.SemaphoreType.DMA
    half = pltpu.VMEM((width, width), BF16)
    tiled = pltpu.VMEM((2, tiles, lanes, width), BF16)
    block = pltpu.VMEM((2, chips * q, rows_b, width), BF16)
    out = pl.pallas_call(
        functools.partial(kernel, n, chips, parts, cuts),
        out_shape=jax.ShapeDtypeStruct((rows_t * tiles, lanes), F32),
        in_specs=[pl.BlockSpec(memory_space=pltpu.HBM)] * 2,
        out_specs=pl.BlockSpec(memory_space=pl.ANY),
        scratch_shapes=[
            pltpu.VMEM((width * tiles, lanes), F32), half, half,
            pltpu.VMEM((2, width, width), F32), tiled, tiled, block, block,
            pltpu.VMEM((chips - 1, q, tiles, rows_b, lanes), F32),
            pltpu.VMEM((chips - 1, q, tiles, rows_b, lanes), F32),
            pltpu.VMEM((q, tiles, rows_b, lanes), F32), pltpu.VMEM((rows_t * tiles, lanes), F32),
            dma((2,)), dma((1,)),
            dma((reach, cuts)), dma((reach, cuts)), dma((reach, cuts)), dma((reach, cuts)),
            dma((reach + 1, 2, cuts)), dma((reach + 1, 2, cuts)),
            dma((chips - 1, parts)), dma((chips - 1, parts)),
            dma((chips, parts)), dma((chips, parts)),
            dma((chips - 1, q, tiles)), dma((chips - 1, q, tiles)),
        ],
        compiler_params=pltpu.CompilerParams(
            collective_id=0, has_side_effects=True, vmem_limit_bytes=40 << 20
        ),
    )(amplitudes.reshape(rows_t * tiles, lanes), fitting.reshape(rows_b, width))
    return out.reshape(rows_t, pair_dev, width)


def solution(mesh):
    spec = P("aux", "pair", None)
    return jax.shard_map(
        functools.partial(per_device, mesh.shape["pair"], mesh.shape["aux"]),
        mesh=mesh, in_specs=(spec, spec), out_specs=spec, check_vma=False,
    )
```

```python
import functools

import jax
import jax.numpy as jnp
from jax import lax
from jax.experimental import pallas as pl
from jax.experimental.pallas import tpu as pltpu
from jax.sharding import PartitionSpec as P

MESH = pl.DeviceIdType.MESH
CUTS, PARTS = 2, 8
F32, BF16 = jnp.float32, jnp.bfloat16
NT = (((1,), (1,)), ((), ()))


def ring_order(n):
    depth = 4 if n % 4 == 0 and n > 4 else 2
    width = n // depth
    if n % 2 or width < 2:
        return list(range(n))
    walk = []
    for z in range(depth):
        ys = range(1, width) if z % 2 == 0 else range(width - 1, 0, -1)
        walk += [z * width + y for y in ys]
    return walk + [z * width for z in range(depth - 1, -1, -1)]


def lookup(table, key):
    return sum(jnp.where(key == k, v, 0) for k, v in enumerate(table))


def split(v):
    high = v.astype(BF16).astype(F32)
    return high, v - high


def kernel(
    n, chips, parts, cuts,
    t_in, b_in, out,
    t_all, t_high, t_low, b_all, b_high, b_low, g_high, g_low,
    outbox, inbox, mine, final,
    local_sem, out_sem, right_send, right_recv, left_send, left_recv, bm_send, bm_recv,
    tx_send, tx_recv, tm_send, tm_recv, px_send, px_recv,
):
    rows_b, width = b_in.shape
    lanes = t_in.shape[1]
    tiles = width // lanes
    rows_t = t_in.shape[0] // tiles
    piece = rows_t // parts
    q = rows_t // rows_b
    reach = n // 2
    order = ring_order(n)
    where = [order.index(k) for k in range(n)]
    pair, aux = lax.axis_index("pair"), lax.axis_index("aux")
    chip, core = aux // 2, aux % 2
    mate = chip * 2 + (1 - core)
    spot = lookup(where, pair)

    def at(step):
        return lookup(order, lax.rem(spot + step + n, n))

    right, left = at(1), at(-1)

    def chip_at(step):
        return lax.rem(chip + step + chips, chips)

    barrier = pltpu.get_barrier_semaphore()
    greet = [(right, aux), (left, aux), (pair, mate)]
    greet += [(pair, chip_at(e) * 2 + core) for e in range(1, chips)]
    for who in greet:
        pl.semaphore_signal(barrier, inc=1, device_id=who, device_id_type=MESH)
    pl.semaphore_wait(barrier, len(greet))

    sizes = [rows_b] if cuts == 1 else [(rows_b // 2 + 15) // 16 * 16, rows_b - (rows_b // 2 + 15) // 16 * 16]
    starts = [0, sizes[0]][:cuts]
    rounds = [(d, g) for d in range(1, reach) for g in range(cuts)] + [(reach, 0)]
    place, due, filled = {}, {}, [rows_b]
    for h in range(cuts):
        place[0, True, h] = place[0, False, h] = starts[h]
        due[0, True, h] = due[0, False, h] = 0

    def carried(d, from_left):
        return d < reach or cuts > 1 or from_left

    def cut_of(g, from_left):
        return g if from_left else cuts - 1 - g

    for v, (d, g) in enumerate(rounds, 1):
        count = filled[-1]
        for from_left in (True, False):
            if carried(d, from_left):
                h = cut_of(g, from_left)
                place[d, from_left, h], due[d, from_left, h] = count, v
                if d == reach:
                    place[d, not from_left, h], due[d, not from_left, h] = count, v
                count += sizes[h]
        filled.append(count)
    n_events = len(filled)
    first = min(cuts + 1, n_events - 1)
    for d in range(reach + 1):
        events = [due[d, side, h] for side in (True, False) for h in range(cuts)]
        if min(events) <= first < max(events):
            for side in (True, False):
                for h in range(cuts):
                    due[d, side, h] = max(events)

    def b_rows(d, from_left, h):
        return pl.ds(place[d, from_left, h], sizes[h])

    def t_rows(owner, s):
        start = (owner * rows_t + s * piece) * tiles
        return pl.ds(pl.multiple_of(start, 8), piece * tiles)

    def t_own(s):
        return pl.ds(s * piece * tiles, piece * tiles)

    def b_source(d, from_left, h):
        return b_in.at[pl.ds(starts[h], sizes[h])] if d == 0 else b_all.at[core, b_rows(d, from_left, h)]

    def hop(d, g, to_right):
        h = cut_of(g, to_right)
        send, recv = (right_send, right_recv) if to_right else (left_send, left_recv)
        return pltpu.make_async_remote_copy(
            src_ref=b_source(d - 1, to_right, h),
            dst_ref=b_all.at[core, b_rows(d, to_right, h)],
            send_sem=send.at[d - 1, h],
            recv_sem=recv.at[d - 1, h],
            device_id=(right if to_right else left, aux),
            device_id_type=MESH,
        )

    def arrive(d, g, from_left):
        h = cut_of(g, from_left)
        rows = b_rows(d, from_left, h)
        send, recv = (right_send, right_recv) if from_left else (left_send, left_recv)
        pltpu.make_async_remote_copy(
            src_ref=b_all.at[core, rows],
            dst_ref=b_all.at[core, rows],
            send_sem=send.at[d - 1, h],
            recv_sem=recv.at[d - 1, h],
            device_id=(left if from_left else right, aux),
            device_id_type=MESH,
        ).wait_recv()

    def b_mate(d, h, from_left, level):
        rows = b_rows(d, from_left, h)
        side = 0 if from_left else 1
        return pltpu.make_async_remote_copy(
            src_ref=b_source(d, from_left, h) if d == 0 else b_all.at[level, rows],
            dst_ref=b_all.at[level, rows],
            send_sem=bm_send.at[d, side, h],
            recv_sem=bm_recv.at[d, side, h],
            device_id=(pair, mate),
            device_id_type=MESH,
        )

    def t_cross(e, s):
        return pltpu.make_async_remote_copy(
            src_ref=t_in.at[t_own(s)],
            dst_ref=t_all.at[t_rows(aux, s)],
            send_sem=tx_send.at[e - 1, s],
            recv_sem=tx_recv.at[e - 1, s],
            device_id=(pair, chip_at(e) * 2 + core),
            device_id_type=MESH,
        )

    def t_mate(e, s):
        rows = t_rows(chip_at(-e) * 2 + core, s)
        return pltpu.make_async_remote_copy(
            src_ref=t_in.at[t_own(s)] if e == 0 else t_all.at[rows],
            dst_ref=t_all.at[rows],
            send_sem=tm_send.at[e, s],
            recv_sem=tm_recv.at[e, s],
            device_id=(pair, mate),
            device_id_type=MESH,
        )

    def t_landed(owner, s, send, recv):
        rows = t_rows(owner, s)
        pltpu.make_async_remote_copy(
            src_ref=t_all.at[rows], dst_ref=t_all.at[rows], send_sem=send, recv_sem=recv,
            device_id=(pair, mate), device_id_type=MESH,
        ).wait_recv()

    started = []

    def go(copy):
        copy.start()
        started.append(copy)

    for s in range(parts):
        for e in range(1, chips):
            go(t_cross(e, s))
        if s == 0:
            for g in range(cuts if reach > 1 else 1):
                for to_right in (True, False):
                    if carried(1, to_right):
                        go(hop(1, g, to_right))
    own_b = pltpu.make_async_copy(
        b_in, b_all.at[core, pl.ds(0, rows_b)], local_sem.at[0]
    )
    own_t = pltpu.make_async_copy(
        t_in, t_all.at[pl.ds(pl.multiple_of(aux * rows_t * tiles, 8), rows_t * tiles)], local_sem.at[1]
    )
    own_t.start()
    own_b.start()
    for s in range(parts):
        go(t_mate(0, s))
    for h in range(cuts):
        go(b_mate(0, h, True, core))

    aligned = piece % 16 == 0

    def t_split(start, size):
        rows = pl.ds(pl.multiple_of(start, 16), size)
        for k in range(tiles):
            high, low = split(t_all[pl.ds(start * tiles + k, size, stride=tiles), :])
            t_high[rows, k * lanes:(k + 1) * lanes] = high.astype(BF16)
            t_low[rows, k * lanes:(k + 1) * lanes] = low.astype(BF16)

    def t_part(owner, s):
        if aligned:
            t_split(owner * rows_t + s * piece, piece)

    def t_over(e, s):
        owner = chip_at(-e) * 2 + (1 - core)
        t_landed(owner, s, tm_send.at[e, s], tm_recv.at[e, s])
        t_part(owner, s)

    def relay(v):
        d, g = rounds[v - 1]
        for from_left in (True, False):
            if carried(d, from_left):
                arrive(d, g, from_left)
                if d + 1 < reach or (d + 1 == reach and g == 0 and carried(reach, from_left)):
                    go(hop(d + 1, g, from_left))
                go(b_mate(d, cut_of(g, from_left), from_left, core))

    def b_over(v):
        if v == 0:
            for h in range(cuts):
                b_mate(0, h, True, 1 - core).wait_recv()
            return
        d, g = rounds[v - 1]
        for from_left in (True, False):
            if carried(d, from_left):
                b_mate(d, cut_of(g, from_left), from_left, 1 - core).wait_recv()

    def t_step(s):
        for e in range(1, chips):
            owner = chip_at(-e) * 2 + core
            t_landed(owner, s, tx_send.at[e - 1, s], tx_recv.at[e - 1, s])
            go(t_mate(e, s))
            t_part(owner, s)
        if s:
            for e in range(1, chips):
                t_over(e, s - 1)

    own_t.wait()
    if aligned:
        @pl.loop(0, parts)
        def _(s):
            t_part(aux, s)

        for s in range(parts):
            t_over(0, s)
    else:
        for s in range(parts):
            t_over(0, s)
    own_b.wait()

    def first_block(slot):
        return (chip_at(slot // q) * 2 + core) * q + lax.rem(slot, q)

    def reach_of(o):
        return (o, False) if o <= reach and o < n - o else (n - o, True)

    def about(table, slot, h):
        away = lax.rem(lookup(where, first_block(slot)) - spot + n, n)
        return lookup([table[reach_of(o) + (h,)] for o in range(n)], away)

    ready = [[about(due, slot, h) for h in range(cuts)] for slot in range(chips * q)]
    origin = [[about(place, slot, h) for h in range(cuts)] for slot in range(chips * q)]

    def pick(table, slot, h):
        return lookup([row[h] for row in table], slot)

    def extent(h):
        return (starts[h], sizes[h]) if h is not None else (0, rows_b)

    def g_part(slot, h):
        start, count = extent(h)
        size = 2 * count
        cuts_in = range(cuts) if h is None else [h]
        pieces = []
        for level in range(2):
            parts_in = [b_all[level, pl.ds(pl.multiple_of(pick(origin, slot, c), 8), sizes[c]), :] for c in cuts_in]
            pieces.append(split(jnp.concatenate(parts_in, axis=0) if len(parts_in) > 1 else parts_in[0]))
        high = jnp.concatenate([p[0] for p in pieces], axis=0)
        low = jnp.concatenate([p[1] for p in pieces], axis=0)
        both = jnp.concatenate([high, low], axis=0).astype(BF16)
        main = jnp.dot(both, t_high[...], preferred_element_type=F32)
        rest = jnp.dot(high.astype(BF16), t_low[...], preferred_element_type=F32)
        high, low = split(main[:size] + (main[size:] + rest))
        for level in range(2):
            part = slice(level * count, (level + 1) * count)
            lane = slice(level * width, (level + 1) * width)
            g_high[slot, start:start + count, lane] = high[part].astype(BF16)
            g_low[slot, start:start + count, lane] = low[part].astype(BF16)

    def product(high, low, cols_high, cols_low):
        rows = high.shape[0]
        dot = functools.partial(lax.dot_general, dimension_numbers=NT, preferred_element_type=F32)
        if rows_b % 16 == 0:
            main = dot(jnp.concatenate([high, low], axis=0), cols_high)
            return main[:rows] + (main[rows:] + dot(high, cols_low))
        return dot(high, cols_high) + (dot(low, cols_high) + dot(high, cols_low))

    def columns(j, count):
        return [ref[pl.ds(j, count)].reshape(count * lanes, 2 * width) for ref in (b_high, b_low)]

    def p_cross(e, i, h, j):
        rows = pl.ds(pl.multiple_of(i * rows_b + starts[h], 8), sizes[h])
        return pltpu.make_async_remote_copy(
            src_ref=outbox.at[e - 1, j, rows], dst_ref=inbox.at[e - 1, j, rows],
            send_sem=px_send.at[e - 1, i, h, j], recv_sem=px_recv.at[e - 1, i, h, j],
            device_id=(pair, chip_at(e) * 2 + core), device_id_type=MESH,
        )

    def full(v):
        return filled[v] // lanes

    def older(v, j):
        @pl.loop(1, chips)
        def _(e):
            old = [[pick(ready, e * q + i, h) < v for h in range(cuts)] for i in range(q)]
            any_old = functools.reduce(jnp.logical_or, [x for row in old for x in row])

            @pl.when(any_old)
            def _():
                if rows_b % 16 == 0:
                    left = [ref[pl.ds(e * q, q)].reshape(q * rows_b, 2 * width) for ref in (g_high, g_low)]
                    outbox[e - 1, j] = product(*left, *columns(j, 1))
                else:
                    for i in range(q):
                        outbox[e - 1, j, i * rows_b:(i + 1) * rows_b] = product(
                            g_high[e * q + i], g_low[e * q + i], *columns(j, 1))
                for i in range(q):
                    for h in range(cuts):
                        @pl.when(old[i][h])
                        def _(i=i, h=h):
                            p_cross(e, i, h, j).start()

    def block_ready(slot):
        return functools.reduce(jnp.maximum, [pick(ready, slot, h) for h in range(cuts)])

    slots = chips * q
    swaps = [jnp.where(block_ready(e * q + 1) < block_ready(e * q), 1, 0) if q == 2 else 0 for e in range(chips)]

    def slot_of(turn):
        if chips == 2 and q == 2:
            e = 1 - lax.rem(turn, 2)
            return e * q + lax.rem(turn // 2 + lookup(swaps, e), 2)
        return lax.rem(turn + q, slots)

    def newer(h, count, wanted, low=0, high=slots):
        start, size = extent(h)

        @pl.loop(low, high)
        def _(turn):
            slot = slot_of(turn)
            e, i = slot // q, lax.rem(slot, q)

            @pl.when(wanted(slot))
            def _():
                g_part(slot, h)

                @pl.when(e > 0)
                def _():
                    rows = pl.ds(pl.multiple_of(i * rows_b + start, 8), size)
                    left = [ref[slot, start:start + size, :] for ref in (g_high, g_low)]

                    def some(j, k):
                        value = product(*left, *columns(j, k))
                        for t in range(k):
                            outbox[e - 1, j + t, rows] = value[:, t * lanes:(t + 1) * lanes]
                            for c in range(cuts) if h is None else [h]:
                                p_cross(e, i, c, j + t).start()

                    if count // 2:
                        @pl.loop(0, count // 2)
                        def _(k):
                            some(2 * k, 2)
                    if count % 2:
                        some(count - 1, 1)

    def tile_split(j):
        for level in range(2):
            high, low = split(b_all[level, pl.ds(j * lanes, lanes), :])
            b_high[j, :, level * width:(level + 1) * width] = high.astype(BF16)
            b_low[j, :, level * width:(level + 1) * width] = low.astype(BF16)

    def prepare(v):
        b_over(v)
        for j in range(full(v - 1) if v else 0, full(v)):
            tile_split(j)

    prepare(0)
    step = 0
    for v in range(1, first + 1):
        upto = parts * (2 * v - 1) // (2 * first)
        for s in range(step, upto):
            t_step(s)
        step = upto
        relay(v)
        if v > 1:
            prepare(v - 1)
    for s in range(step, parts):
        t_step(s)
    if first + 1 < n_events:
        relay(first + 1)
    for e in range(1, chips):
        t_over(e, parts - 1)
    if not aligned:
        @pl.loop(0, width // 128)
        def _(i):
            t_split(i * 128, 128)
    prepare(first)

    own_last = functools.reduce(jnp.maximum, [ready[i][h] for i in range(q) for h in range(cuts)])

    def own_columns(j, count):
        if rows_b % 16 == 0:
            left = [ref[:q].reshape(q * rows_b, 2 * width) for ref in (g_high, g_low)]
            value = product(*left, *columns(j, count))
            for k in range(count):
                mine[j + k] = value[:, k * lanes:(k + 1) * lanes]
        else:
            for k in range(count):
                @pl.loop(0, q)
                def _(i):
                    mine[j + k, pl.ds(pl.multiple_of(i * rows_b, 8), rows_b)] = product(
                        g_high[i], g_low[i], *columns(j + k, 1))

    def own_pairs(low, high):
        @pl.loop(low, high)
        def _(k):
            own_columns(2 * k, 2)

    def begun(slot):
        return block_ready(slot) <= first

    newer(None, full(first), begun, 0, slots // 2)
    if first + 2 < n_events:
        relay(first + 2)
    newer(None, full(first), begun, slots // 2, slots)
    halfway = min(first + 2, n_events - 1)
    early_pairs = full(halfway) // 2
    for v in range(first + 1, n_events):
        if v > first + 2:
            relay(v)
        prepare(v)
        for j in range(full(v - 1), full(v)):
            older(v, j)
        if cuts == 1 or v == n_events - 1 or v == first + 1:
            newer(None, full(v), lambda slot: block_ready(slot) == v)
        else:
            for h in range(cuts):
                newer(h, full(v), lambda slot: pick(ready, slot, h) == v)
        if v == halfway:
            @pl.when(own_last <= v)
            def _():
                own_pairs(0, early_pairs)

    if halfway > first:
        @pl.when(own_last > halfway)
        def _():
            own_pairs(0, early_pairs)

        own_pairs(early_pairs, tiles // 2)
    else:
        own_pairs(0, tiles // 2)
    if tiles % 2:
        own_columns(tiles - 1, 1)

    def block_of(d, from_left):
        return at(-d if from_left else d)

    segments = [[] for _ in range(tiles)]
    seen = set()
    for (d, from_left, h), begin in sorted(place.items(), key=lambda item: item[1]):
        if begin in seen:
            continue
        seen.add(begin)
        for j in range(begin // lanes, (begin + sizes[h] - 1) // lanes + 1):
            low, high = max(begin, j * lanes), min(begin + sizes[h], (j + 1) * lanes)
            segments[j].append((low - j * lanes, high - low, d, from_left, starts[h] + low - begin))

    lane = lax.broadcasted_iota(jnp.int32, (1, lanes), 1)

    for j in range(tiles):
        for e in range(1, chips):
            for i in range(q):
                for h in range(cuts):
                    p_cross(e, i, h, j).wait_recv()
        total = mine[j]
        for e in range(1, chips):
            total = total + inbox[e - 1, j]
        for begin, size, d, from_left, offset in segments[j]:
            goal = block_of(d, from_left) * rows_b + offset
            turned = pltpu.roll(total, lax.rem(goal - begin + lanes, lanes), 1)
            for part in range(2):
                into = goal // lanes + part
                inside = jnp.logical_and(lane >= goal - into * lanes, lane < goal - into * lanes + size)

                @pl.when(goal + size > into * lanes)
                def _():
                    at_rows = pl.ds(into, rows_t, stride=tiles)
                    final[at_rows, :] = jnp.where(inside, turned, final[at_rows, :])

    done = pltpu.make_async_copy(final, out, out_sem.at[0])
    done.start()
    for copy in started:
        copy.wait_send()
    for e in range(1, chips):
        for i in range(q):
            for h in range(cuts):
                for j in range(tiles):
                    p_cross(e, i, h, j).wait_send()
    done.wait()


def per_device(n, n_aux, amplitudes, fitting):
    rows_t, pair_dev, width = amplitudes.shape
    count_fit, rows_b, _ = fitting.shape
    assert pair_dev == 1 and count_fit == 1 and rows_t % rows_b == 0
    chips = n_aux // 2
    parts = max([p for p in range(1, PARTS + 1) if rows_t % (16 * p) == 0], default=1)
    cuts = CUTS if rows_b % 16 == 0 and n > 2 else 1
    reach = n // 2
    lanes = 128
    tiles = width // lanes
    q = rows_t // rows_b
    dma = pltpu.SemaphoreType.DMA
    half = pltpu.VMEM((width, width), BF16)
    tiled = pltpu.VMEM((tiles, lanes, 2 * width), BF16)
    block = pltpu.VMEM((chips * q, rows_b, 2 * width), BF16)
    out = pl.pallas_call(
        functools.partial(kernel, n, chips, parts, cuts),
        out_shape=jax.ShapeDtypeStruct((rows_t * tiles, lanes), F32),
        in_specs=[pl.BlockSpec(memory_space=pltpu.HBM)] * 2,
        out_specs=pl.BlockSpec(memory_space=pl.ANY),
        scratch_shapes=[
            pltpu.VMEM((width * tiles, lanes), F32), half, half,
            pltpu.VMEM((2, width, width), F32), tiled, tiled, block, block,
            pltpu.VMEM((chips - 1, tiles, q * rows_b, lanes), F32),
            pltpu.VMEM((chips - 1, tiles, q * rows_b, lanes), F32),
            pltpu.VMEM((tiles, q * rows_b, lanes), F32), pltpu.VMEM((rows_t * tiles, lanes), F32),
            dma((2,)), dma((1,)),
            dma((reach, cuts)), dma((reach, cuts)), dma((reach, cuts)), dma((reach, cuts)),
            dma((reach + 1, 2, cuts)), dma((reach + 1, 2, cuts)),
            dma((chips - 1, parts)), dma((chips - 1, parts)),
            dma((chips, parts)), dma((chips, parts)),
            dma((chips - 1, q, cuts, tiles)), dma((chips - 1, q, cuts, tiles)),
        ],
        compiler_params=pltpu.CompilerParams(
            collective_id=0, has_side_effects=True, vmem_limit_bytes=40 << 20
        ),
    )(amplitudes.reshape(rows_t * tiles, lanes), fitting.reshape(rows_b, width))
    return out.reshape(rows_t, pair_dev, width)


def solution(mesh):
    spec = P("aux", "pair", None)
    return jax.shard_map(
        functools.partial(per_device, mesh.shape["pair"], mesh.shape["aux"]),
        mesh=mesh, in_specs=(spec, spec), out_specs=spec, check_vma=False,
    )
```

```python
import functools

import jax
import jax.numpy as jnp
from jax import lax
from jax.experimental import pallas as pl
from jax.experimental.pallas import tpu as pltpu
from jax.sharding import PartitionSpec as P

MESH = pl.DeviceIdType.MESH
CUTS, PARTS = 2, 8
F32, BF16 = jnp.float32, jnp.bfloat16
NT = (((1,), (1,)), ((), ()))


def ring_order(n):
    depth = 4 if n % 4 == 0 and n > 4 else 2
    width = n // depth
    if n % 2 or width < 2:
        return list(range(n))
    walk = []
    for z in range(depth):
        ys = range(1, width) if z % 2 == 0 else range(width - 1, 0, -1)
        walk += [z * width + y for y in ys]
    return walk + [z * width for z in range(depth - 1, -1, -1)]


def lookup(table, key):
    return sum(jnp.where(key == k, v, 0) for k, v in enumerate(table))


def split(v):
    high = v.astype(BF16).astype(F32)
    return high, v - high


def kernel(
    n, chips, parts, cuts,
    t_in, b_in, out,
    t_all, t_high, t_low, b_all, b_high, b_low, g_high, g_low,
    outbox, inbox, mine, final, g_ahead,
    local_sem, out_sem, right_send, right_recv, left_send, left_recv, bm_send, bm_recv,
    tx_send, tx_recv, tm_send, tm_recv, px_send, px_recv,
):
    rows_b, width = b_in.shape
    lanes = t_in.shape[1]
    tiles = width // lanes
    rows_t = t_in.shape[0] // tiles
    piece = rows_t // parts
    q = rows_t // rows_b
    reach = n // 2
    order = ring_order(n)
    where = [order.index(k) for k in range(n)]
    pair, aux = lax.axis_index("pair"), lax.axis_index("aux")
    chip, core = aux // 2, aux % 2
    mate = chip * 2 + (1 - core)
    spot = lookup(where, pair)

    def at(step):
        return lookup(order, lax.rem(spot + step + n, n))

    right, left = at(1), at(-1)

    def chip_at(step):
        return lax.rem(chip + step + chips, chips)

    barrier = pltpu.get_barrier_semaphore()
    greet = [(right, aux), (left, aux), (pair, mate)]
    greet += [(pair, chip_at(e) * 2 + core) for e in range(1, chips)]
    for who in greet:
        pl.semaphore_signal(barrier, inc=1, device_id=who, device_id_type=MESH)
    pl.semaphore_wait(barrier, len(greet))

    sizes = [rows_b] if cuts == 1 else [(rows_b // 2 + 15) // 16 * 16, rows_b - (rows_b // 2 + 15) // 16 * 16]
    starts = [0, sizes[0]][:cuts]
    rounds = [(d, g) for d in range(1, reach) for g in range(cuts)] + [(reach, 0)]
    place, due, filled = {}, {}, [rows_b]
    for h in range(cuts):
        place[0, True, h] = place[0, False, h] = starts[h]
        due[0, True, h] = due[0, False, h] = 0

    def carried(d, from_left):
        return d < reach or cuts > 1 or from_left

    def cut_of(g, from_left):
        return g if from_left else cuts - 1 - g

    for v, (d, g) in enumerate(rounds, 1):
        count = filled[-1]
        for from_left in (True, False):
            if carried(d, from_left):
                h = cut_of(g, from_left)
                place[d, from_left, h], due[d, from_left, h] = count, v
                if d == reach:
                    place[d, not from_left, h], due[d, not from_left, h] = count, v
                count += sizes[h]
        filled.append(count)
    n_events = len(filled)
    first = min(cuts + 1, n_events - 1)
    for d in range(reach + 1):
        events = [due[d, side, h] for side in (True, False) for h in range(cuts)]
        if min(events) <= first < max(events):
            for side in (True, False):
                for h in range(cuts):
                    due[d, side, h] = max(events)

    def b_rows(d, from_left, h):
        return pl.ds(place[d, from_left, h], sizes[h])

    def t_rows(owner, s):
        start = (owner * rows_t + s * piece) * tiles
        return pl.ds(pl.multiple_of(start, 8), piece * tiles)

    def t_own(s):
        return pl.ds(s * piece * tiles, piece * tiles)

    def b_source(d, from_left, h):
        return b_in.at[pl.ds(starts[h], sizes[h])] if d == 0 else b_all.at[core, b_rows(d, from_left, h)]

    def hop(d, g, to_right):
        h = cut_of(g, to_right)
        send, recv = (right_send, right_recv) if to_right else (left_send, left_recv)
        return pltpu.make_async_remote_copy(
            src_ref=b_source(d - 1, to_right, h),
            dst_ref=b_all.at[core, b_rows(d, to_right, h)],
            send_sem=send.at[d - 1, h],
            recv_sem=recv.at[d - 1, h],
            device_id=(right if to_right else left, aux),
            device_id_type=MESH,
        )

    def arrive(d, g, from_left):
        h = cut_of(g, from_left)
        rows = b_rows(d, from_left, h)
        send, recv = (right_send, right_recv) if from_left else (left_send, left_recv)
        pltpu.make_async_remote_copy(
            src_ref=b_all.at[core, rows],
            dst_ref=b_all.at[core, rows],
            send_sem=send.at[d - 1, h],
            recv_sem=recv.at[d - 1, h],
            device_id=(left if from_left else right, aux),
            device_id_type=MESH,
        ).wait_recv()

    def b_mate(d, h, from_left, level):
        rows = b_rows(d, from_left, h)
        side = 0 if from_left else 1
        return pltpu.make_async_remote_copy(
            src_ref=b_source(d, from_left, h) if d == 0 else b_all.at[level, rows],
            dst_ref=b_all.at[level, rows],
            send_sem=bm_send.at[d, side, h],
            recv_sem=bm_recv.at[d, side, h],
            device_id=(pair, mate),
            device_id_type=MESH,
        )

    def t_cross(e, s):
        return pltpu.make_async_remote_copy(
            src_ref=t_in.at[t_own(s)],
            dst_ref=t_all.at[t_rows(aux, s)],
            send_sem=tx_send.at[e - 1, s],
            recv_sem=tx_recv.at[e - 1, s],
            device_id=(pair, chip_at(e) * 2 + core),
            device_id_type=MESH,
        )

    def t_mate(e, s):
        rows = t_rows(chip_at(-e) * 2 + core, s)
        return pltpu.make_async_remote_copy(
            src_ref=t_in.at[t_own(s)] if e == 0 else t_all.at[rows],
            dst_ref=t_all.at[rows],
            send_sem=tm_send.at[e, s],
            recv_sem=tm_recv.at[e, s],
            device_id=(pair, mate),
            device_id_type=MESH,
        )

    def t_landed(owner, s, send, recv):
        rows = t_rows(owner, s)
        pltpu.make_async_remote_copy(
            src_ref=t_all.at[rows], dst_ref=t_all.at[rows], send_sem=send, recv_sem=recv,
            device_id=(pair, mate), device_id_type=MESH,
        ).wait_recv()

    started = []

    def go(copy):
        copy.start()
        started.append(copy)

    for s in range(parts):
        for e in range(1, chips):
            go(t_cross(e, s))
        if s == 0:
            for g in range(cuts if reach > 1 else 1):
                for to_right in (True, False):
                    if carried(1, to_right):
                        go(hop(1, g, to_right))
    own_b = pltpu.make_async_copy(
        b_in, b_all.at[core, pl.ds(0, rows_b)], local_sem.at[0]
    )
    own_t = pltpu.make_async_copy(
        t_in, t_all.at[pl.ds(pl.multiple_of(aux * rows_t * tiles, 8), rows_t * tiles)], local_sem.at[1]
    )
    own_t.start()
    own_b.start()
    for s in range(parts):
        go(t_mate(0, s))
    for h in range(cuts):
        go(b_mate(0, h, True, core))

    aligned = piece % 16 == 0

    def t_split(start, size):
        rows = pl.ds(pl.multiple_of(start, 16), size)
        for k in range(tiles):
            high, low = split(t_all[pl.ds(start * tiles + k, size, stride=tiles), :])
            t_high[rows, k * lanes:(k + 1) * lanes] = high.astype(BF16)
            t_low[rows, k * lanes:(k + 1) * lanes] = low.astype(BF16)

    def t_part(owner, s):
        if aligned:
            t_split(owner * rows_t + s * piece, piece)

    def t_over(e, s):
        owner = chip_at(-e) * 2 + (1 - core)
        t_landed(owner, s, tm_send.at[e, s], tm_recv.at[e, s])
        t_part(owner, s)

    def relay(v):
        d, g = rounds[v - 1]
        for from_left in (True, False):
            if carried(d, from_left):
                arrive(d, g, from_left)
                if d + 1 < reach or (d + 1 == reach and g == 0 and carried(reach, from_left)):
                    go(hop(d + 1, g, from_left))
                go(b_mate(d, cut_of(g, from_left), from_left, core))

    def b_over(v):
        if v == 0:
            for h in range(cuts):
                b_mate(0, h, True, 1 - core).wait_recv()
            return
        d, g = rounds[v - 1]
        for from_left in (True, False):
            if carried(d, from_left):
                b_mate(d, cut_of(g, from_left), from_left, 1 - core).wait_recv()

    def t_step(s):
        for e in range(1, chips):
            owner = chip_at(-e) * 2 + core
            t_landed(owner, s, tx_send.at[e - 1, s], tx_recv.at[e - 1, s])
            go(t_mate(e, s))
            t_part(owner, s)
        if s:
            for e in range(1, chips):
                t_over(e, s - 1)

    own_t.wait()
    if aligned:
        @pl.loop(0, parts)
        def _(s):
            t_part(aux, s)

        for s in range(parts):
            t_over(0, s)
    else:
        for s in range(parts):
            t_over(0, s)
    own_b.wait()

    def first_block(slot):
        return (chip_at(slot // q) * 2 + core) * q + lax.rem(slot, q)

    def reach_of(o):
        return (o, False) if o <= reach and o < n - o else (n - o, True)

    def about(table, slot, h):
        away = lax.rem(lookup(where, first_block(slot)) - spot + n, n)
        return lookup([table[reach_of(o) + (h,)] for o in range(n)], away)

    ready = [[about(due, slot, h) for h in range(cuts)] for slot in range(chips * q)]
    origin = [[about(place, slot, h) for h in range(cuts)] for slot in range(chips * q)]

    def pick(table, slot, h):
        return lookup([row[h] for row in table], slot)

    def extent(h):
        return (starts[h], sizes[h]) if h is not None else (0, rows_b)

    ahead = (2 * rows_t // lanes) if chips == 2 and aligned else 0
    near = pl.ds(pl.multiple_of(chip * (tiles - ahead) * lanes, lanes), ahead * lanes)
    rest_of = pl.ds(pl.multiple_of((1 - chip) * ahead * lanes, lanes), (tiles - ahead) * lanes)

    def g_sum(slot, h, span):
        count = extent(h)[1]
        cuts_in = range(cuts) if h is None else [h]
        pieces = []
        for level in range(2):
            parts_in = [
                b_all[level, pl.ds(pl.multiple_of(pick(origin, slot, c), 8), sizes[c]), span] for c in cuts_in
            ]
            pieces.append(split(jnp.concatenate(parts_in, axis=0) if len(parts_in) > 1 else parts_in[0]))
        high = jnp.concatenate([p[0] for p in pieces], axis=0)
        low = jnp.concatenate([p[1] for p in pieces], axis=0)
        both = jnp.concatenate([high, low], axis=0).astype(BF16)
        main = jnp.dot(both, t_high[span, :], preferred_element_type=F32)
        rest = jnp.dot(high.astype(BF16), t_low[span, :], preferred_element_type=F32)
        return main[:2 * count] + (main[2 * count:] + rest)

    def g_part(slot, h, begun_before=False):
        start, count = extent(h)
        if begun_before:
            total = g_ahead[slot] + g_sum(slot, h, rest_of)
        else:
            total = g_sum(slot, h, slice(None))
        high, low = split(total)
        for level in range(2):
            part = slice(level * count, (level + 1) * count)
            lane = slice(level * width, (level + 1) * width)
            g_high[slot, start:start + count, lane] = high[part].astype(BF16)
            g_low[slot, start:start + count, lane] = low[part].astype(BF16)

    def product(high, low, cols_high, cols_low):
        rows = high.shape[0]
        dot = functools.partial(lax.dot_general, dimension_numbers=NT, preferred_element_type=F32)
        if rows_b % 16 == 0:
            main = dot(jnp.concatenate([high, low], axis=0), cols_high)
            return main[:rows] + (main[rows:] + dot(high, cols_low))
        return dot(high, cols_high) + (dot(low, cols_high) + dot(high, cols_low))

    def columns(j, count):
        return [ref[pl.ds(j, count)].reshape(count * lanes, 2 * width) for ref in (b_high, b_low)]

    def p_cross(e, i, h, j):
        rows = pl.ds(pl.multiple_of(i * rows_b + starts[h], 8), sizes[h])
        return pltpu.make_async_remote_copy(
            src_ref=outbox.at[e - 1, j, rows], dst_ref=inbox.at[e - 1, j, rows],
            send_sem=px_send.at[e - 1, i, h, j], recv_sem=px_recv.at[e - 1, i, h, j],
            device_id=(pair, chip_at(e) * 2 + core), device_id_type=MESH,
        )

    def full(v):
        return filled[v] // lanes

    def older(v, j):
        @pl.loop(1, chips)
        def _(e):
            old = [[pick(ready, e * q + i, h) < v for h in range(cuts)] for i in range(q)]
            any_old = functools.reduce(jnp.logical_or, [x for row in old for x in row])

            @pl.when(any_old)
            def _():
                if rows_b % 16 == 0:
                    left = [ref[pl.ds(e * q, q)].reshape(q * rows_b, 2 * width) for ref in (g_high, g_low)]
                    outbox[e - 1, j] = product(*left, *columns(j, 1))
                else:
                    for i in range(q):
                        outbox[e - 1, j, i * rows_b:(i + 1) * rows_b] = product(
                            g_high[e * q + i], g_low[e * q + i], *columns(j, 1))
                for i in range(q):
                    for h in range(cuts):
                        @pl.when(old[i][h])
                        def _(i=i, h=h):
                            p_cross(e, i, h, j).start()

    def block_ready(slot):
        return functools.reduce(jnp.maximum, [pick(ready, slot, h) for h in range(cuts)])

    slots = chips * q
    swaps = [jnp.where(block_ready(e * q + 1) < block_ready(e * q), 1, 0) if q == 2 else 0 for e in range(chips)]

    def slot_of(turn):
        if chips == 2 and q == 2:
            e = 1 - lax.rem(turn, 2)
            return e * q + lax.rem(turn // 2 + lookup(swaps, e), 2)
        return lax.rem(turn + q, slots)

    def newer(h, count, wanted, low=0, high=slots, begun_before=False):
        start, size = extent(h)

        @pl.loop(low, high)
        def _(turn):
            slot = slot_of(turn)
            e, i = slot // q, lax.rem(slot, q)

            @pl.when(wanted(slot))
            def _():
                g_part(slot, h, begun_before)

                @pl.when(e > 0)
                def _():
                    rows = pl.ds(pl.multiple_of(i * rows_b + start, 8), size)
                    left = [ref[slot, start:start + size, :] for ref in (g_high, g_low)]

                    def some(j, k):
                        value = product(*left, *columns(j, k))
                        for t in range(k):
                            outbox[e - 1, j + t, rows] = value[:, t * lanes:(t + 1) * lanes]
                            for c in range(cuts) if h is None else [h]:
                                p_cross(e, i, c, j + t).start()

                    if count // 2:
                        @pl.loop(0, count // 2)
                        def _(k):
                            some(2 * k, 2)
                    if count % 2:
                        some(count - 1, 1)

    def tile_split(j):
        for level in range(2):
            high, low = split(b_all[level, pl.ds(j * lanes, lanes), :])
            b_high[j, :, level * width:(level + 1) * width] = high.astype(BF16)
            b_low[j, :, level * width:(level + 1) * width] = low.astype(BF16)

    def prepare(v):
        b_over(v)
        for j in range(full(v - 1) if v else 0, full(v)):
            tile_split(j)

    def begun(slot):
        return block_ready(slot) <= first

    assert all(v < first for (d, _, _), v in due.items() if v <= first) or not ahead
    prepare(0)
    step = 0
    for v in range(1, first + 1):
        upto = parts * (2 * v - 1) // (2 * first)
        for s in range(step, upto):
            t_step(s)
        step = upto
        relay(v)
        if v > 1:
            prepare(v - 1)
    if ahead:
        @pl.loop(0, slots)
        def _(turn):
            slot = slot_of(turn)

            @pl.when(begun(slot))
            def _():
                g_ahead[slot] = g_sum(slot, None, near)

    for s in range(step, parts):
        t_step(s)
    if first + 1 < n_events:
        relay(first + 1)
    for e in range(1, chips):
        t_over(e, parts - 1)
    if not aligned:
        @pl.loop(0, width // 128)
        def _(i):
            t_split(i * 128, 128)
    prepare(first)

    own_last = functools.reduce(jnp.maximum, [ready[i][h] for i in range(q) for h in range(cuts)])

    def own_columns(j, count):
        if rows_b % 16 == 0:
            left = [ref[:q].reshape(q * rows_b, 2 * width) for ref in (g_high, g_low)]
            value = product(*left, *columns(j, count))
            for k in range(count):
                mine[j + k] = value[:, k * lanes:(k + 1) * lanes]
        else:
            for k in range(count):
                @pl.loop(0, q)
                def _(i):
                    mine[j + k, pl.ds(pl.multiple_of(i * rows_b, 8), rows_b)] = product(
                        g_high[i], g_low[i], *columns(j + k, 1))

    def own_pairs(low, high):
        @pl.loop(low, high)
        def _(k):
            own_columns(2 * k, 2)

    newer(None, full(first), begun, 0, slots // 2, bool(ahead))
    if first + 2 < n_events:
        relay(first + 2)
    newer(None, full(first), begun, slots // 2, slots, bool(ahead))
    halfway = min(first + 2, n_events - 1)
    early_pairs = full(halfway) // 2
    for v in range(first + 1, n_events):
        if v > first + 2:
            relay(v)
        prepare(v)
        for j in range(full(v - 1), full(v)):
            older(v, j)
        if cuts == 1 or v == n_events - 1 or v == first + 1:
            newer(None, full(v), lambda slot: block_ready(slot) == v)
        else:
            for h in range(cuts):
                newer(h, full(v), lambda slot: pick(ready, slot, h) == v)
        if v == halfway:
            @pl.when(own_last <= v)
            def _():
                own_pairs(0, early_pairs)

    if halfway > first:
        @pl.when(own_last > halfway)
        def _():
            own_pairs(0, early_pairs)

        own_pairs(early_pairs, tiles // 2)
    else:
        own_pairs(0, tiles // 2)
    if tiles % 2:
        own_columns(tiles - 1, 1)

    def block_of(d, from_left):
        return at(-d if from_left else d)

    segments = [[] for _ in range(tiles)]
    seen = set()
    for (d, from_left, h), begin in sorted(place.items(), key=lambda item: item[1]):
        if begin in seen:
            continue
        seen.add(begin)
        for j in range(begin // lanes, (begin + sizes[h] - 1) // lanes + 1):
            low, high = max(begin, j * lanes), min(begin + sizes[h], (j + 1) * lanes)
            segments[j].append((low - j * lanes, high - low, d, from_left, starts[h] + low - begin))

    lane = lax.broadcasted_iota(jnp.int32, (1, lanes), 1)

    for j in range(tiles):
        for e in range(1, chips):
            for i in range(q):
                for h in range(cuts):
                    p_cross(e, i, h, j).wait_recv()
        total = mine[j]
        for e in range(1, chips):
            total = total + inbox[e - 1, j]
        for begin, size, d, from_left, offset in segments[j]:
            goal = block_of(d, from_left) * rows_b + offset
            turned = pltpu.roll(total, lax.rem(goal - begin + lanes, lanes), 1)
            for part in range(2):
                into = goal // lanes + part
                inside = jnp.logical_and(lane >= goal - into * lanes, lane < goal - into * lanes + size)

                @pl.when(goal + size > into * lanes)
                def _():
                    at_rows = pl.ds(into, rows_t, stride=tiles)
                    final[at_rows, :] = jnp.where(inside, turned, final[at_rows, :])

    done = pltpu.make_async_copy(final, out, out_sem.at[0])
    done.start()
    for copy in started:
        copy.wait_send()
    for e in range(1, chips):
        for i in range(q):
            for h in range(cuts):
                for j in range(tiles):
                    p_cross(e, i, h, j).wait_send()
    done.wait()


def per_device(n, n_aux, amplitudes, fitting):
    rows_t, pair_dev, width = amplitudes.shape
    count_fit, rows_b, _ = fitting.shape
    assert pair_dev == 1 and count_fit == 1 and rows_t % rows_b == 0
    chips = n_aux // 2
    parts = max([p for p in range(1, PARTS + 1) if rows_t % (16 * p) == 0], default=1)
    cuts = CUTS if rows_b % 16 == 0 and n > 2 else 1
    reach = n // 2
    lanes = 128
    tiles = width // lanes
    q = rows_t // rows_b
    dma = pltpu.SemaphoreType.DMA
    half = pltpu.VMEM((width, width), BF16)
    tiled = pltpu.VMEM((tiles, lanes, 2 * width), BF16)
    block = pltpu.VMEM((chips * q, rows_b, 2 * width), BF16)
    out = pl.pallas_call(
        functools.partial(kernel, n, chips, parts, cuts),
        out_shape=jax.ShapeDtypeStruct((rows_t * tiles, lanes), F32),
        in_specs=[pl.BlockSpec(memory_space=pltpu.HBM)] * 2,
        out_specs=pl.BlockSpec(memory_space=pl.ANY),
        scratch_shapes=[
            pltpu.VMEM((width * tiles, lanes), F32), half, half,
            pltpu.VMEM((2, width, width), F32), tiled, tiled, block, block,
            pltpu.VMEM((chips - 1, tiles, q * rows_b, lanes), F32),
            pltpu.VMEM((chips - 1, tiles, q * rows_b, lanes), F32),
            pltpu.VMEM((tiles, q * rows_b, lanes), F32), pltpu.VMEM((rows_t * tiles, lanes), F32),
            pltpu.VMEM((chips * q, 2 * rows_b, width), F32),
            dma((2,)), dma((1,)),
            dma((reach, cuts)), dma((reach, cuts)), dma((reach, cuts)), dma((reach, cuts)),
            dma((reach + 1, 2, cuts)), dma((reach + 1, 2, cuts)),
            dma((chips - 1, parts)), dma((chips - 1, parts)),
            dma((chips, parts)), dma((chips, parts)),
            dma((chips - 1, q, cuts, tiles)), dma((chips - 1, q, cuts, tiles)),
        ],
        compiler_params=pltpu.CompilerParams(
            collective_id=0, has_side_effects=True, vmem_limit_bytes=105 << 19
        ),
    )(amplitudes.reshape(rows_t * tiles, lanes), fitting.reshape(rows_b, width))
    return out.reshape(rows_t, pair_dev, width)


def solution(mesh):
    spec = P("aux", "pair", None)
    return jax.shard_map(
        functools.partial(per_device, mesh.shape["pair"], mesh.shape["aux"]),
        mesh=mesh, in_specs=(spec, spec), out_specs=spec, check_vma=False,
    )
```

```python
import functools

import jax
import jax.numpy as jnp
from jax import lax
from jax.experimental import pallas as pl
from jax.experimental.pallas import tpu as pltpu
from jax.sharding import PartitionSpec as P

MESH = pl.DeviceIdType.MESH
CUTS, PARTS = 2, 8
F32, BF16 = jnp.float32, jnp.bfloat16
NT = (((1,), (1,)), ((), ()))


def ring_order(n):
    depth = 4 if n % 4 == 0 and n > 4 else 2
    width = n // depth
    if n % 2 or width < 2:
        return list(range(n))
    walk = []
    for z in range(depth):
        ys = range(1, width) if z % 2 == 0 else range(width - 1, 0, -1)
        walk += [z * width + y for y in ys]
    return walk + [z * width for z in range(depth - 1, -1, -1)]


def lookup(table, key):
    return sum(jnp.where(key == k, v, 0) for k, v in enumerate(table))


def split(v):
    high = v.astype(BF16).astype(F32)
    return high, v - high


def kernel(
    n, chips, parts, cuts,
    t_in, b_in, out,
    t_all, t_high, t_low, b_all, b_high, b_low, g_high, g_low,
    outbox, inbox, mine, final, g_ahead,
    local_sem, out_sem, right_send, right_recv, left_send, left_recv, bm_send, bm_recv,
    tx_send, tx_recv, tm_send, tm_recv, px_send, px_recv,
):
    rows_b, width = b_in.shape
    lanes = t_in.shape[1]
    tiles = width // lanes
    rows_t = t_in.shape[0] // tiles
    piece = rows_t // parts
    q = rows_t // rows_b
    reach = n // 2
    order = ring_order(n)
    where = [order.index(k) for k in range(n)]
    pair, aux = lax.axis_index("pair"), lax.axis_index("aux")
    chip, core = aux // 2, aux % 2
    mate = chip * 2 + (1 - core)
    spot = lookup(where, pair)

    def at(step):
        return lookup(order, lax.rem(spot + step + n, n))

    right, left = at(1), at(-1)

    def chip_at(step):
        return lax.rem(chip + step + chips, chips)

    barrier = pltpu.get_barrier_semaphore()
    greet = [(right, aux), (left, aux), (pair, mate)]
    greet += [(pair, chip_at(e) * 2 + core) for e in range(1, chips)]
    for who in greet:
        pl.semaphore_signal(barrier, inc=1, device_id=who, device_id_type=MESH)
    pl.semaphore_wait(barrier, len(greet))

    sizes = [rows_b] if cuts == 1 else [(rows_b // 2 + 15) // 16 * 16, rows_b - (rows_b // 2 + 15) // 16 * 16]
    starts = [0, sizes[0]][:cuts]
    rounds = [(d, g) for d in range(1, reach) for g in range(cuts)] + [(reach, 0)]
    place, due, filled = {}, {}, [rows_b]
    for h in range(cuts):
        place[0, True, h] = place[0, False, h] = starts[h]
        due[0, True, h] = due[0, False, h] = 0

    def carried(d, from_left):
        return d < reach or cuts > 1 or from_left

    def cut_of(g, from_left):
        return g if from_left else cuts - 1 - g

    for v, (d, g) in enumerate(rounds, 1):
        count = filled[-1]
        for from_left in (True, False):
            if carried(d, from_left):
                h = cut_of(g, from_left)
                place[d, from_left, h], due[d, from_left, h] = count, v
                if d == reach:
                    place[d, not from_left, h], due[d, not from_left, h] = count, v
                count += sizes[h]
        filled.append(count)
    n_events = len(filled)
    first = min(cuts + 1, n_events - 1)
    for d in range(reach + 1):
        events = [due[d, side, h] for side in (True, False) for h in range(cuts)]
        if min(events) <= first < max(events):
            for side in (True, False):
                for h in range(cuts):
                    due[d, side, h] = max(events)

    def b_rows(d, from_left, h):
        return pl.ds(place[d, from_left, h], sizes[h])

    def t_rows(owner, s):
        start = (owner * rows_t + s * piece) * tiles
        return pl.ds(pl.multiple_of(start, 8), piece * tiles)

    def t_own(s):
        return pl.ds(s * piece * tiles, piece * tiles)

    def b_source(d, from_left, h):
        return b_in.at[pl.ds(starts[h], sizes[h])] if d == 0 else b_all.at[core, b_rows(d, from_left, h)]

    def hop(d, g, to_right):
        h = cut_of(g, to_right)
        send, recv = (right_send, right_recv) if to_right else (left_send, left_recv)
        return pltpu.make_async_remote_copy(
            src_ref=b_source(d - 1, to_right, h),
            dst_ref=b_all.at[core, b_rows(d, to_right, h)],
            send_sem=send.at[d - 1, h],
            recv_sem=recv.at[d - 1, h],
            device_id=(right if to_right else left, aux),
            device_id_type=MESH,
        )

    def arrive(d, g, from_left):
        h = cut_of(g, from_left)
        rows = b_rows(d, from_left, h)
        send, recv = (right_send, right_recv) if from_left else (left_send, left_recv)
        pltpu.make_async_remote_copy(
            src_ref=b_all.at[core, rows],
            dst_ref=b_all.at[core, rows],
            send_sem=send.at[d - 1, h],
            recv_sem=recv.at[d - 1, h],
            device_id=(left if from_left else right, aux),
            device_id_type=MESH,
        ).wait_recv()

    def b_mate(d, h, from_left, level):
        rows = b_rows(d, from_left, h)
        side = 0 if from_left else 1
        return pltpu.make_async_remote_copy(
            src_ref=b_source(d, from_left, h) if d == 0 else b_all.at[level, rows],
            dst_ref=b_all.at[level, rows],
            send_sem=bm_send.at[d, side, h],
            recv_sem=bm_recv.at[d, side, h],
            device_id=(pair, mate),
            device_id_type=MESH,
        )

    def t_cross(e, s):
        return pltpu.make_async_remote_copy(
            src_ref=t_in.at[t_own(s)],
            dst_ref=t_all.at[t_rows(aux, s)],
            send_sem=tx_send.at[e - 1, s],
            recv_sem=tx_recv.at[e - 1, s],
            device_id=(pair, chip_at(e) * 2 + core),
            device_id_type=MESH,
        )

    def t_mate(e, s):
        rows = t_rows(chip_at(-e) * 2 + core, s)
        return pltpu.make_async_remote_copy(
            src_ref=t_in.at[t_own(s)] if e == 0 else t_all.at[rows],
            dst_ref=t_all.at[rows],
            send_sem=tm_send.at[e, s],
            recv_sem=tm_recv.at[e, s],
            device_id=(pair, mate),
            device_id_type=MESH,
        )

    def t_landed(owner, s, send, recv):
        rows = t_rows(owner, s)
        pltpu.make_async_remote_copy(
            src_ref=t_all.at[rows], dst_ref=t_all.at[rows], send_sem=send, recv_sem=recv,
            device_id=(pair, mate), device_id_type=MESH,
        ).wait_recv()

    started = []

    def go(copy):
        copy.start()
        started.append(copy)

    for s in range(parts):
        for e in range(1, chips):
            go(t_cross(e, s))
        if s == 0:
            for g in range(cuts if reach > 1 else 1):
                for to_right in (True, False):
                    if carried(1, to_right):
                        go(hop(1, g, to_right))
    own_b = pltpu.make_async_copy(
        b_in, b_all.at[core, pl.ds(0, rows_b)], local_sem.at[0]
    )
    own_t = pltpu.make_async_copy(
        t_in, t_all.at[pl.ds(pl.multiple_of(aux * rows_t * tiles, 8), rows_t * tiles)], local_sem.at[1]
    )
    own_t.start()
    own_b.start()
    for s in range(parts):
        go(t_mate(0, s))
    for h in range(cuts):
        go(b_mate(0, h, True, core))

    aligned = piece % 16 == 0

    def t_split(start, size):
        rows = pl.ds(pl.multiple_of(start, 16), size)
        for k in range(tiles):
            high, low = split(t_all[pl.ds(start * tiles + k, size, stride=tiles), :])
            t_high[rows, k * lanes:(k + 1) * lanes] = high.astype(BF16)
            t_low[rows, k * lanes:(k + 1) * lanes] = low.astype(BF16)

    def t_part(owner, s):
        if aligned:
            t_split(owner * rows_t + s * piece, piece)

    def t_over(e, s):
        owner = chip_at(-e) * 2 + (1 - core)
        t_landed(owner, s, tm_send.at[e, s], tm_recv.at[e, s])
        t_part(owner, s)

    def relay(v):
        d, g = rounds[v - 1]
        for from_left in (True, False):
            if carried(d, from_left):
                arrive(d, g, from_left)
                if d + 1 < reach or (d + 1 == reach and g == 0 and carried(reach, from_left)):
                    go(hop(d + 1, g, from_left))
                go(b_mate(d, cut_of(g, from_left), from_left, core))

    def b_over(v):
        if v == 0:
            for h in range(cuts):
                b_mate(0, h, True, 1 - core).wait_recv()
            return
        d, g = rounds[v - 1]
        for from_left in (True, False):
            if carried(d, from_left):
                b_mate(d, cut_of(g, from_left), from_left, 1 - core).wait_recv()

    def t_step(s):
        for e in range(1, chips):
            owner = chip_at(-e) * 2 + core
            t_landed(owner, s, tx_send.at[e - 1, s], tx_recv.at[e - 1, s])
            go(t_mate(e, s))
            t_part(owner, s)
        if s:
            for e in range(1, chips):
                t_over(e, s - 1)

    own_t.wait()
    if aligned:
        @pl.loop(0, parts)
        def _(s):
            t_part(aux, s)

        for s in range(parts):
            t_over(0, s)
    else:
        for s in range(parts):
            t_over(0, s)
    own_b.wait()

    def first_block(slot):
        return (chip_at(slot // q) * 2 + core) * q + lax.rem(slot, q)

    def reach_of(o):
        return (o, False) if o <= reach and o < n - o else (n - o, True)

    def about(table, slot, h):
        away = lax.rem(lookup(where, first_block(slot)) - spot + n, n)
        return lookup([table[reach_of(o) + (h,)] for o in range(n)], away)

    ready = [[about(due, slot, h) for h in range(cuts)] for slot in range(chips * q)]
    origin = [[about(place, slot, h) for h in range(cuts)] for slot in range(chips * q)]

    def pick(table, slot, h):
        return lookup([row[h] for row in table], slot)

    def extent(h):
        return (starts[h], sizes[h]) if h is not None else (0, rows_b)

    ahead = (2 * rows_t // lanes) if chips == 2 and aligned else 0
    near = pl.ds(pl.multiple_of(chip * (tiles - ahead) * lanes, lanes), ahead * lanes)
    rest_of = pl.ds(pl.multiple_of((1 - chip) * ahead * lanes, lanes), (tiles - ahead) * lanes)

    def g_sum(slot, h, span):
        count = extent(h)[1]
        cuts_in = range(cuts) if h is None else [h]
        pieces = []
        for level in range(2):
            parts_in = [
                b_all[level, pl.ds(pl.multiple_of(pick(origin, slot, c), 8), sizes[c]), span] for c in cuts_in
            ]
            pieces.append(split(jnp.concatenate(parts_in, axis=0) if len(parts_in) > 1 else parts_in[0]))
        high = jnp.concatenate([p[0] for p in pieces], axis=0)
        low = jnp.concatenate([p[1] for p in pieces], axis=0)
        both = jnp.concatenate([high, low], axis=0).astype(BF16)
        main = jnp.dot(both, t_high[span, :], preferred_element_type=F32)
        rest = jnp.dot(high.astype(BF16), t_low[span, :], preferred_element_type=F32)
        return main[:2 * count] + (main[2 * count:] + rest)

    def g_part(slot, h, begun_before=False):
        start, count = extent(h)
        if begun_before:
            total = g_ahead[slot] + g_sum(slot, h, rest_of)
        else:
            total = g_sum(slot, h, slice(None))
        high, low = split(total)
        for level in range(2):
            part = slice(level * count, (level + 1) * count)
            lane = slice(level * width, (level + 1) * width)
            g_high[slot, start:start + count, lane] = high[part].astype(BF16)
            g_low[slot, start:start + count, lane] = low[part].astype(BF16)

    def product(high, low, cols_high, cols_low):
        rows = high.shape[0]
        dot = functools.partial(lax.dot_general, dimension_numbers=NT, preferred_element_type=F32)
        if rows_b % 16 == 0:
            main = dot(jnp.concatenate([high, low], axis=0), cols_high)
            return main[:rows] + (main[rows:] + dot(high, cols_low))
        return dot(high, cols_high) + (dot(low, cols_high) + dot(high, cols_low))

    def columns(j, count):
        return [ref[pl.ds(j, count)].reshape(count * lanes, 2 * width) for ref in (b_high, b_low)]

    def p_cross(e, i, h, j):
        rows = pl.ds(pl.multiple_of(i * rows_b + starts[h], 8), sizes[h])
        return pltpu.make_async_remote_copy(
            src_ref=outbox.at[e - 1, j, rows], dst_ref=inbox.at[e - 1, j, rows],
            send_sem=px_send.at[e - 1, i, h, j], recv_sem=px_recv.at[e - 1, i, h, j],
            device_id=(pair, chip_at(e) * 2 + core), device_id_type=MESH,
        )

    def full(v):
        return filled[v] // lanes

    def older(v, j):
        @pl.loop(1, chips)
        def _(e):
            old = [[pick(ready, e * q + i, h) < v for h in range(cuts)] for i in range(q)]
            any_old = functools.reduce(jnp.logical_or, [x for row in old for x in row])

            @pl.when(any_old)
            def _():
                if rows_b % 16 == 0:
                    left = [ref[pl.ds(e * q, q)].reshape(q * rows_b, 2 * width) for ref in (g_high, g_low)]
                    outbox[e - 1, j] = product(*left, *columns(j, 1))
                else:
                    for i in range(q):
                        outbox[e - 1, j, i * rows_b:(i + 1) * rows_b] = product(
                            g_high[e * q + i], g_low[e * q + i], *columns(j, 1))
                for i in range(q):
                    for h in range(cuts):
                        @pl.when(old[i][h])
                        def _(i=i, h=h):
                            p_cross(e, i, h, j).start()

    def block_ready(slot):
        return functools.reduce(jnp.maximum, [pick(ready, slot, h) for h in range(cuts)])

    slots = chips * q
    swaps = [jnp.where(block_ready(e * q + 1) < block_ready(e * q), 1, 0) if q == 2 else 0 for e in range(chips)]

    def slot_of(turn):
        if chips == 2 and q == 2:
            e = 1 - lax.rem(turn, 2)
            return e * q + lax.rem(turn // 2 + lookup(swaps, e), 2)
        return lax.rem(turn + q, slots)

    def newer(h, count, wanted, low=0, high=slots, begun_before=False):
        start, size = extent(h)

        @pl.loop(low, high)
        def _(turn):
            slot = slot_of(turn)
            e, i = slot // q, lax.rem(slot, q)

            @pl.when(wanted(slot))
            def _():
                g_part(slot, h, begun_before)

                @pl.when(e > 0)
                def _():
                    rows = pl.ds(pl.multiple_of(i * rows_b + start, 8), size)
                    left = [ref[slot, start:start + size, :] for ref in (g_high, g_low)]

                    def some(j, k):
                        value = product(*left, *columns(j, k))
                        for t in range(k):
                            outbox[e - 1, j + t, rows] = value[:, t * lanes:(t + 1) * lanes]
                            for c in range(cuts) if h is None else [h]:
                                p_cross(e, i, c, j + t).start()

                    if count // 2:
                        @pl.loop(0, count // 2)
                        def _(k):
                            some(2 * k, 2)
                    if count % 2:
                        some(count - 1, 1)

    def tile_split(j):
        for level in range(2):
            high, low = split(b_all[level, pl.ds(j * lanes, lanes), :])
            b_high[j, :, level * width:(level + 1) * width] = high.astype(BF16)
            b_low[j, :, level * width:(level + 1) * width] = low.astype(BF16)

    def prepare(v):
        b_over(v)
        for j in range(full(v - 1) if v else 0, full(v)):
            tile_split(j)

    def begun(slot):
        return block_ready(slot) <= first

    assert all(v < first for (d, _, _), v in due.items() if v <= first) or not ahead
    prepare(0)
    step = 0
    for v in range(1, first + 1):
        upto = parts * (2 * v - 1) // (2 * first)
        for s in range(step, upto):
            t_step(s)
        step = upto
        relay(v)
        if v > 1:
            prepare(v - 1)
    if ahead:
        @pl.loop(0, slots)
        def _(turn):
            slot = slot_of(turn)

            @pl.when(begun(slot))
            def _():
                g_ahead[slot] = g_sum(slot, None, near)

    for s in range(step, parts):
        t_step(s)
    if first + 1 < n_events:
        relay(first + 1)
    for e in range(1, chips):
        t_over(e, parts - 1)
    if not aligned:
        @pl.loop(0, width // 128)
        def _(i):
            t_split(i * 128, 128)
    prepare(first)

    own_last = functools.reduce(jnp.maximum, [ready[i][h] for i in range(q) for h in range(cuts)])

    def own_columns(j, count):
        if rows_b % 16 == 0:
            left = [ref[:q].reshape(q * rows_b, 2 * width) for ref in (g_high, g_low)]
            value = product(*left, *columns(j, count))
            for k in range(count):
                mine[j + k] = value[:, k * lanes:(k + 1) * lanes]
        else:
            for k in range(count):
                @pl.loop(0, q)
                def _(i):
                    mine[j + k, pl.ds(pl.multiple_of(i * rows_b, 8), rows_b)] = product(
                        g_high[i], g_low[i], *columns(j + k, 1))

    def own_pairs(low, high):
        @pl.loop(low, high)
        def _(k):
            own_columns(2 * k, 2)

    base = min(first + 1, n_events - 1)
    if base > first:
        prepare(base)

    def joined(slot):
        return block_ready(slot) == base

    def group(low, high):
        newer(None, full(base), begun, low, high, bool(ahead))
        if base > first:
            newer(None, full(base), joined, low, high)

    group(0, slots // 2)
    if first + 2 < n_events:
        relay(first + 2)
    group(slots // 2, slots)
    halfway = min(first + 2, n_events - 1)
    early_pairs = full(halfway) // 2
    for v in range(base + 1, n_events):
        if v > first + 2:
            relay(v)
        prepare(v)
        for j in range(full(v - 1), full(v)):
            older(v, j)
        if cuts == 1 or v == n_events - 1:
            newer(None, full(v), lambda slot: block_ready(slot) == v)
        else:
            for h in range(cuts):
                newer(h, full(v), lambda slot: pick(ready, slot, h) == v)
        if v == halfway:
            @pl.when(own_last <= v)
            def _():
                own_pairs(0, early_pairs)

    if halfway > base:
        @pl.when(own_last > halfway)
        def _():
            own_pairs(0, early_pairs)

        own_pairs(early_pairs, tiles // 2)
    else:
        own_pairs(0, tiles // 2)
    if tiles % 2:
        own_columns(tiles - 1, 1)

    def block_of(d, from_left):
        return at(-d if from_left else d)

    segments = [[] for _ in range(tiles)]
    seen = set()
    for (d, from_left, h), begin in sorted(place.items(), key=lambda item: item[1]):
        if begin in seen:
            continue
        seen.add(begin)
        for j in range(begin // lanes, (begin + sizes[h] - 1) // lanes + 1):
            low, high = max(begin, j * lanes), min(begin + sizes[h], (j + 1) * lanes)
            segments[j].append((low - j * lanes, high - low, d, from_left, starts[h] + low - begin))

    lane = lax.broadcasted_iota(jnp.int32, (1, lanes), 1)

    for j in range(tiles):
        for e in range(1, chips):
            for i in range(q):
                for h in range(cuts):
                    p_cross(e, i, h, j).wait_recv()
        total = mine[j]
        for e in range(1, chips):
            total = total + inbox[e - 1, j]
        for begin, size, d, from_left, offset in segments[j]:
            goal = block_of(d, from_left) * rows_b + offset
            turned = pltpu.roll(total, lax.rem(goal - begin + lanes, lanes), 1)
            for part in range(2):
                into = goal // lanes + part
                inside = jnp.logical_and(lane >= goal - into * lanes, lane < goal - into * lanes + size)

                @pl.when(goal + size > into * lanes)
                def _():
                    at_rows = pl.ds(into, rows_t, stride=tiles)
                    final[at_rows, :] = jnp.where(inside, turned, final[at_rows, :])

    done = pltpu.make_async_copy(final, out, out_sem.at[0])
    done.start()
    for copy in started:
        copy.wait_send()
    for e in range(1, chips):
        for i in range(q):
            for h in range(cuts):
                for j in range(tiles):
                    p_cross(e, i, h, j).wait_send()
    done.wait()


def per_device(n, n_aux, amplitudes, fitting):
    rows_t, pair_dev, width = amplitudes.shape
    count_fit, rows_b, _ = fitting.shape
    assert pair_dev == 1 and count_fit == 1 and rows_t % rows_b == 0
    chips = n_aux // 2
    parts = max([p for p in range(1, PARTS + 1) if rows_t % (16 * p) == 0], default=1)
    cuts = CUTS if rows_b % 16 == 0 and n > 2 else 1
    reach = n // 2
    lanes = 128
    tiles = width // lanes
    q = rows_t // rows_b
    dma = pltpu.SemaphoreType.DMA
    half = pltpu.VMEM((width, width), BF16)
    tiled = pltpu.VMEM((tiles, lanes, 2 * width), BF16)
    block = pltpu.VMEM((chips * q, rows_b, 2 * width), BF16)
    out = pl.pallas_call(
        functools.partial(kernel, n, chips, parts, cuts),
        out_shape=jax.ShapeDtypeStruct((rows_t * tiles, lanes), F32),
        in_specs=[pl.BlockSpec(memory_space=pltpu.HBM)] * 2,
        out_specs=pl.BlockSpec(memory_space=pl.ANY),
        scratch_shapes=[
            pltpu.VMEM((width * tiles, lanes), F32), half, half,
            pltpu.VMEM((2, width, width), F32), tiled, tiled, block, block,
            pltpu.VMEM((chips - 1, tiles, q * rows_b, lanes), F32),
            pltpu.VMEM((chips - 1, tiles, q * rows_b, lanes), F32),
            pltpu.VMEM((tiles, q * rows_b, lanes), F32), pltpu.VMEM((rows_t * tiles, lanes), F32),
            pltpu.VMEM((chips * q, 2 * rows_b, width), F32),
            dma((2,)), dma((1,)),
            dma((reach, cuts)), dma((reach, cuts)), dma((reach, cuts)), dma((reach, cuts)),
            dma((reach + 1, 2, cuts)), dma((reach + 1, 2, cuts)),
            dma((chips - 1, parts)), dma((chips - 1, parts)),
            dma((chips, parts)), dma((chips, parts)),
            dma((chips - 1, q, cuts, tiles)), dma((chips - 1, q, cuts, tiles)),
        ],
        compiler_params=pltpu.CompilerParams(
            collective_id=0, has_side_effects=True, vmem_limit_bytes=105 << 19
        ),
    )(amplitudes.reshape(rows_t * tiles, lanes), fitting.reshape(rows_b, width))
    return out.reshape(rows_t, pair_dev, width)


def solution(mesh):
    spec = P("aux", "pair", None)
    return jax.shard_map(
        functools.partial(per_device, mesh.shape["pair"], mesh.shape["aux"]),
        mesh=mesh, in_specs=(spec, spec), out_specs=spec, check_vma=False,
    )
```

```python
import functools

import jax
import jax.numpy as jnp
from jax import lax
from jax.experimental import pallas as pl
from jax.experimental.pallas import tpu as pltpu
from jax.sharding import PartitionSpec as P

MESH = pl.DeviceIdType.MESH
CUTS, PARTS = 2, 8
F32, BF16 = jnp.float32, jnp.bfloat16
NT = (((1,), (1,)), ((), ()))


def ring_order(n):
    depth = 4 if n % 4 == 0 and n > 4 else 2
    width = n // depth
    if n % 2 or width < 2:
        return list(range(n))
    walk = []
    for z in range(depth):
        ys = range(1, width) if z % 2 == 0 else range(width - 1, 0, -1)
        walk += [z * width + y for y in ys]
    return walk + [z * width for z in range(depth - 1, -1, -1)]


def lookup(table, key):
    return sum(jnp.where(key == k, v, 0) for k, v in enumerate(table))


def split(v):
    high = v.astype(BF16).astype(F32)
    return high, v - high


def kernel(
    n, chips, parts, cuts,
    t_in, b_in, out,
    t_all, t_high, t_low, b_all, b_high, b_low, g_high, g_low,
    outbox, inbox, mine, final, g_ahead,
    local_sem, out_sem, right_send, right_recv, left_send, left_recv, bm_send, bm_recv,
    tx_send, tx_recv, tm_send, tm_recv, px_send, px_recv,
):
    rows_b, width = b_in.shape
    lanes = t_in.shape[1]
    tiles = width // lanes
    rows_t = t_in.shape[0] // tiles
    piece = rows_t // parts
    q = rows_t // rows_b
    reach = n // 2
    order = ring_order(n)
    where = [order.index(k) for k in range(n)]
    pair, aux = lax.axis_index("pair"), lax.axis_index("aux")
    chip, core = aux // 2, aux % 2
    mate = chip * 2 + (1 - core)
    spot = lookup(where, pair)

    def at(step):
        return lookup(order, lax.rem(spot + step + n, n))

    right, left = at(1), at(-1)

    def chip_at(step):
        return lax.rem(chip + step + chips, chips)

    barrier = pltpu.get_barrier_semaphore()
    greet = [(right, aux), (left, aux), (pair, mate)]
    greet += [(pair, chip_at(e) * 2 + core) for e in range(1, chips)]
    for who in greet:
        pl.semaphore_signal(barrier, inc=1, device_id=who, device_id_type=MESH)
    pl.semaphore_wait(barrier, len(greet))

    sizes = [rows_b] if cuts == 1 else [(rows_b // 2 + 15) // 16 * 16, rows_b - (rows_b // 2 + 15) // 16 * 16]
    starts = [0, sizes[0]][:cuts]
    rounds = [(d, g) for d in range(1, reach) for g in range(cuts)] + [(reach, 0)]
    place, due, filled = {}, {}, [rows_b]
    for h in range(cuts):
        place[0, True, h] = place[0, False, h] = starts[h]
        due[0, True, h] = due[0, False, h] = 0

    def carried(d, from_left):
        return d < reach or cuts > 1 or from_left

    def cut_of(g, from_left):
        return g if from_left else cuts - 1 - g

    for v, (d, g) in enumerate(rounds, 1):
        count = filled[-1]
        for from_left in (True, False):
            if carried(d, from_left):
                h = cut_of(g, from_left)
                place[d, from_left, h], due[d, from_left, h] = count, v
                if d == reach:
                    place[d, not from_left, h], due[d, not from_left, h] = count, v
                count += sizes[h]
        filled.append(count)
    n_events = len(filled)
    first = min(cuts + 1, n_events - 1)
    for d in range(reach + 1):
        events = [due[d, side, h] for side in (True, False) for h in range(cuts)]
        if min(events) <= first < max(events):
            for side in (True, False):
                for h in range(cuts):
                    due[d, side, h] = max(events)

    def b_rows(d, from_left, h):
        return pl.ds(place[d, from_left, h], sizes[h])

    def t_rows(owner, s):
        start = (owner * rows_t + s * piece) * tiles
        return pl.ds(pl.multiple_of(start, 8), piece * tiles)

    def t_own(s):
        return pl.ds(s * piece * tiles, piece * tiles)

    def b_source(d, from_left, h):
        return b_in.at[pl.ds(starts[h], sizes[h])] if d == 0 else b_all.at[core, b_rows(d, from_left, h)]

    def hop(d, g, to_right):
        h = cut_of(g, to_right)
        send, recv = (right_send, right_recv) if to_right else (left_send, left_recv)
        return pltpu.make_async_remote_copy(
            src_ref=b_source(d - 1, to_right, h),
            dst_ref=b_all.at[core, b_rows(d, to_right, h)],
            send_sem=send.at[d - 1, h],
            recv_sem=recv.at[d - 1, h],
            device_id=(right if to_right else left, aux),
            device_id_type=MESH,
        )

    def arrive(d, g, from_left):
        h = cut_of(g, from_left)
        rows = b_rows(d, from_left, h)
        send, recv = (right_send, right_recv) if from_left else (left_send, left_recv)
        pltpu.make_async_remote_copy(
            src_ref=b_all.at[core, rows],
            dst_ref=b_all.at[core, rows],
            send_sem=send.at[d - 1, h],
            recv_sem=recv.at[d - 1, h],
            device_id=(left if from_left else right, aux),
            device_id_type=MESH,
        ).wait_recv()

    def b_mate(d, h, from_left, level):
        rows = b_rows(d, from_left, h)
        side = 0 if from_left else 1
        return pltpu.make_async_remote_copy(
            src_ref=b_source(d, from_left, h) if d == 0 else b_all.at[level, rows],
            dst_ref=b_all.at[level, rows],
            send_sem=bm_send.at[d, side, h],
            recv_sem=bm_recv.at[d, side, h],
            device_id=(pair, mate),
            device_id_type=MESH,
        )

    def t_cross(e, s):
        return pltpu.make_async_remote_copy(
            src_ref=t_in.at[t_own(s)],
            dst_ref=t_all.at[t_rows(aux, s)],
            send_sem=tx_send.at[e - 1, s],
            recv_sem=tx_recv.at[e - 1, s],
            device_id=(pair, chip_at(e) * 2 + core),
            device_id_type=MESH,
        )

    def t_mate(e, s):
        rows = t_rows(chip_at(-e) * 2 + core, s)
        return pltpu.make_async_remote_copy(
            src_ref=t_in.at[t_own(s)] if e == 0 else t_all.at[rows],
            dst_ref=t_all.at[rows],
            send_sem=tm_send.at[e, s],
            recv_sem=tm_recv.at[e, s],
            device_id=(pair, mate),
            device_id_type=MESH,
        )

    def t_landed(owner, s, send, recv):
        rows = t_rows(owner, s)
        pltpu.make_async_remote_copy(
            src_ref=t_all.at[rows], dst_ref=t_all.at[rows], send_sem=send, recv_sem=recv,
            device_id=(pair, mate), device_id_type=MESH,
        ).wait_recv()

    started = []

    def go(copy):
        copy.start()
        started.append(copy)

    for s in range(parts):
        for e in range(1, chips):
            go(t_cross(e, s))
        if s == 0:
            for g in range(cuts if reach > 1 else 1):
                for to_right in (True, False):
                    if carried(1, to_right):
                        go(hop(1, g, to_right))
    own_b = pltpu.make_async_copy(
        b_in, b_all.at[core, pl.ds(0, rows_b)], local_sem.at[0]
    )
    own_t = pltpu.make_async_copy(
        t_in, t_all.at[pl.ds(pl.multiple_of(aux * rows_t * tiles, 8), rows_t * tiles)], local_sem.at[1]
    )
    own_t.start()
    own_b.start()
    for s in range(parts):
        go(t_mate(0, s))
    for h in range(cuts):
        go(b_mate(0, h, True, core))

    aligned = piece % 16 == 0

    def t_split(start, size):
        rows = pl.ds(pl.multiple_of(start, 16), size)
        for k in range(tiles):
            high, low = split(t_all[pl.ds(start * tiles + k, size, stride=tiles), :])
            t_high[rows, k * lanes:(k + 1) * lanes] = high.astype(BF16)
            t_low[rows, k * lanes:(k + 1) * lanes] = low.astype(BF16)

    def t_part(owner, s):
        if aligned:
            t_split(owner * rows_t + s * piece, piece)

    def t_over(e, s):
        owner = chip_at(-e) * 2 + (1 - core)
        t_landed(owner, s, tm_send.at[e, s], tm_recv.at[e, s])
        t_part(owner, s)

    def relay(v):
        d, g = rounds[v - 1]
        for from_left in (True, False):
            if carried(d, from_left):
                arrive(d, g, from_left)
                if d + 1 < reach or (d + 1 == reach and g == 0 and carried(reach, from_left)):
                    go(hop(d + 1, g, from_left))
                go(b_mate(d, cut_of(g, from_left), from_left, core))

    def b_over(v):
        if v == 0:
            for h in range(cuts):
                b_mate(0, h, True, 1 - core).wait_recv()
            return
        d, g = rounds[v - 1]
        for from_left in (True, False):
            if carried(d, from_left):
                b_mate(d, cut_of(g, from_left), from_left, 1 - core).wait_recv()

    def t_step(s):
        for e in range(1, chips):
            owner = chip_at(-e) * 2 + core
            t_landed(owner, s, tx_send.at[e - 1, s], tx_recv.at[e - 1, s])
            go(t_mate(e, s))
            t_part(owner, s)
        if s:
            for e in range(1, chips):
                t_over(e, s - 1)

    own_t.wait()
    if aligned:
        @pl.loop(0, parts)
        def _(s):
            t_part(aux, s)

        for s in range(parts):
            t_over(0, s)
    else:
        for s in range(parts):
            t_over(0, s)
    own_b.wait()

    def first_block(slot):
        return (chip_at(slot // q) * 2 + core) * q + lax.rem(slot, q)

    def reach_of(o):
        return (o, False) if o <= reach and o < n - o else (n - o, True)

    def about(table, slot, h):
        away = lax.rem(lookup(where, first_block(slot)) - spot + n, n)
        return lookup([table[reach_of(o) + (h,)] for o in range(n)], away)

    ready = [[about(due, slot, h) for h in range(cuts)] for slot in range(chips * q)]
    origin = [[about(place, slot, h) for h in range(cuts)] for slot in range(chips * q)]

    def pick(table, slot, h):
        return lookup([row[h] for row in table], slot)

    def extent(h):
        return (starts[h], sizes[h]) if h is not None else (0, rows_b)

    ahead = (2 * rows_t // lanes) if chips == 2 and aligned else 0
    near = pl.ds(pl.multiple_of(chip * (tiles - ahead) * lanes, lanes), ahead * lanes)
    rest_of = pl.ds(pl.multiple_of((1 - chip) * ahead * lanes, lanes), (tiles - ahead) * lanes)

    def g_sum(slot, h, span):
        count = extent(h)[1]
        cuts_in = range(cuts) if h is None else [h]
        pieces = []
        for level in range(2):
            parts_in = [
                b_all[level, pl.ds(pl.multiple_of(pick(origin, slot, c), 8), sizes[c]), span] for c in cuts_in
            ]
            pieces.append(split(jnp.concatenate(parts_in, axis=0) if len(parts_in) > 1 else parts_in[0]))
        high = jnp.concatenate([p[0] for p in pieces], axis=0)
        low = jnp.concatenate([p[1] for p in pieces], axis=0)
        both = jnp.concatenate([high, low], axis=0).astype(BF16)
        main = jnp.dot(both, t_high[span, :], preferred_element_type=F32)
        rest = jnp.dot(high.astype(BF16), t_low[span, :], preferred_element_type=F32)
        return main[:2 * count] + (main[2 * count:] + rest)

    def g_part(slot, h, begun_before=False):
        start, count = extent(h)
        if begun_before:
            total = g_ahead[slot] + g_sum(slot, h, rest_of)
        else:
            total = g_sum(slot, h, slice(None))
        high, low = split(total)
        for level in range(2):
            part = slice(level * count, (level + 1) * count)
            lane = slice(level * width, (level + 1) * width)
            g_high[slot, start:start + count, lane] = high[part].astype(BF16)
            g_low[slot, start:start + count, lane] = low[part].astype(BF16)

    def product(high, low, cols_high, cols_low):
        rows = high.shape[0]
        dot = functools.partial(lax.dot_general, dimension_numbers=NT, preferred_element_type=F32)
        if rows_b % 16 == 0:
            main = dot(jnp.concatenate([high, low], axis=0), cols_high)
            return main[:rows] + (main[rows:] + dot(high, cols_low))
        return dot(high, cols_high) + (dot(low, cols_high) + dot(high, cols_low))

    def columns(j, count):
        return [ref[pl.ds(j, count)].reshape(count * lanes, 2 * width) for ref in (b_high, b_low)]

    def p_cross(e, i, h, j):
        rows = pl.ds(pl.multiple_of(i * rows_b + starts[h], 8), sizes[h])
        return pltpu.make_async_remote_copy(
            src_ref=outbox.at[e - 1, j, rows], dst_ref=inbox.at[e - 1, j, rows],
            send_sem=px_send.at[e - 1, i, h, j], recv_sem=px_recv.at[e - 1, i, h, j],
            device_id=(pair, chip_at(e) * 2 + core), device_id_type=MESH,
        )

    def full(v):
        return filled[v] // lanes

    def older(v, j):
        @pl.loop(q, slots)
        def _(turn):
            slot = slot_of(turn - q)
            e, i = slot // q, lax.rem(slot, q)
            old = [pick(ready, slot, h) < v for h in range(cuts)]

            @pl.when(functools.reduce(jnp.logical_or, old))
            def _():
                rows = pl.ds(pl.multiple_of(i * rows_b, 8), rows_b)
                outbox[e - 1, j, rows] = product(g_high[slot], g_low[slot], *columns(j, 1))
                for h in range(cuts):
                    @pl.when(old[h])
                    def _(h=h):
                        p_cross(e, i, h, j).start()

    def block_ready(slot):
        return functools.reduce(jnp.maximum, [pick(ready, slot, h) for h in range(cuts)])

    slots = chips * q
    swaps = [jnp.where(block_ready(e * q + 1) < block_ready(e * q), 1, 0) if q == 2 else 0 for e in range(chips)]

    def slot_of(turn):
        if chips == 2 and q == 2:
            e = 1 - turn // 2
            return e * q + lax.rem(turn + lookup(swaps, e), 2)
        return lax.rem(turn + q, slots)

    def newer(h, count, wanted, low=0, high=slots, begun_before=False):
        start, size = extent(h)

        @pl.loop(low, high)
        def _(turn):
            slot = slot_of(turn)
            e, i = slot // q, lax.rem(slot, q)

            @pl.when(wanted(slot))
            def _():
                g_part(slot, h, begun_before)

                @pl.when(e > 0)
                def _():
                    rows = pl.ds(pl.multiple_of(i * rows_b + start, 8), size)
                    left = [ref[slot, start:start + size, :] for ref in (g_high, g_low)]

                    def some(j, k):
                        value = product(*left, *columns(j, k))
                        for t in range(k):
                            outbox[e - 1, j + t, rows] = value[:, t * lanes:(t + 1) * lanes]
                            for c in range(cuts) if h is None else [h]:
                                p_cross(e, i, c, j + t).start()

                    if count // 2:
                        @pl.loop(0, count // 2)
                        def _(k):
                            some(2 * k, 2)
                    if count % 2:
                        some(count - 1, 1)

    def tile_split(j):
        for level in range(2):
            high, low = split(b_all[level, pl.ds(j * lanes, lanes), :])
            b_high[j, :, level * width:(level + 1) * width] = high.astype(BF16)
            b_low[j, :, level * width:(level + 1) * width] = low.astype(BF16)

    def prepare(v):
        b_over(v)
        for j in range(full(v - 1) if v else 0, full(v)):
            tile_split(j)

    def begun(slot):
        return block_ready(slot) <= first

    assert all(v < first for (d, _, _), v in due.items() if v <= first) or not ahead
    prepare(0)
    step = 0
    for v in range(1, first + 1):
        upto = parts * (2 * v - 1) // (2 * first)
        for s in range(step, upto):
            t_step(s)
        step = upto
        relay(v)
        if v > 1:
            prepare(v - 1)
    if ahead:
        @pl.loop(0, slots)
        def _(turn):
            slot = slot_of(turn)

            @pl.when(begun(slot))
            def _():
                g_ahead[slot] = g_sum(slot, None, near)

    for s in range(step, parts):
        t_step(s)
    if first + 1 < n_events:
        relay(first + 1)
    for e in range(1, chips):
        t_over(e, parts - 1)
    if not aligned:
        @pl.loop(0, width // 128)
        def _(i):
            t_split(i * 128, 128)
    prepare(first)

    def own_columns(j, count):
        if rows_b % 16 == 0:
            left = [ref[:q].reshape(q * rows_b, 2 * width) for ref in (g_high, g_low)]
            value = product(*left, *columns(j, count))
            for k in range(count):
                mine[j + k] = value[:, k * lanes:(k + 1) * lanes]
        else:
            for k in range(count):
                @pl.loop(0, q)
                def _(i):
                    mine[j + k, pl.ds(pl.multiple_of(i * rows_b, 8), rows_b)] = product(
                        g_high[i], g_low[i], *columns(j + k, 1))

    def own_pairs(low, high):
        @pl.loop(low, high)
        def _(k):
            own_columns(2 * k, 2)

    base = min(first + 1, n_events - 1)
    if base > first:
        prepare(base)

    def joined(slot):
        return block_ready(slot) == base

    late = block_ready(slot_of(slots - q - 1)) > base

    def group(low, high, when=True):
        newer(None, full(base), lambda slot: jnp.logical_and(begun(slot), when), low, high, bool(ahead))
        if base > first:
            newer(None, full(base), lambda slot: jnp.logical_and(joined(slot), when), low, high)

    some = (slots - q + 1) // 2
    most = slots - q + q // 2
    idle = block_ready(slot_of(0)) > base
    group(0, some)
    group(slots - q, slots, idle)
    if first + 2 < n_events:
        relay(first + 2)
    group(some, slots - q)
    group(slots - q, most, jnp.logical_not(idle))
    group(most, slots, jnp.logical_and(late, jnp.logical_not(idle)))
    for v in range(base + 1, n_events):
        if v > first + 2:
            relay(v)
        prepare(v)
        for j in range(full(v - 1), full(v)):
            older(v, j)
        if cuts == 1 or v == n_events - 1:
            newer(None, full(v), lambda slot: block_ready(slot) == v)
        else:
            for h in range(cuts):
                newer(h, full(v), lambda slot: pick(ready, slot, h) == v)

    group(most, slots, jnp.logical_not(jnp.logical_or(idle, late)))
    own_pairs(0, tiles // 2)
    if tiles % 2:
        own_columns(tiles - 1, 1)

    def block_of(d, from_left):
        return at(-d if from_left else d)

    segments = [[] for _ in range(tiles)]
    seen = set()
    for (d, from_left, h), begin in sorted(place.items(), key=lambda item: item[1]):
        if begin in seen:
            continue
        seen.add(begin)
        for j in range(begin // lanes, (begin + sizes[h] - 1) // lanes + 1):
            low, high = max(begin, j * lanes), min(begin + sizes[h], (j + 1) * lanes)
            segments[j].append((low - j * lanes, high - low, d, from_left, starts[h] + low - begin))

    lane = lax.broadcasted_iota(jnp.int32, (1, lanes), 1)

    for j in range(tiles):
        for e in range(1, chips):
            for i in range(q):
                for h in range(cuts):
                    p_cross(e, i, h, j).wait_recv()
        total = mine[j]
        for e in range(1, chips):
            total = total + inbox[e - 1, j]
        for begin, size, d, from_left, offset in segments[j]:
            goal = block_of(d, from_left) * rows_b + offset
            turned = pltpu.roll(total, lax.rem(goal - begin + lanes, lanes), 1)
            for part in range(2):
                into = goal // lanes + part
                inside = jnp.logical_and(lane >= goal - into * lanes, lane < goal - into * lanes + size)

                @pl.when(goal + size > into * lanes)
                def _():
                    at_rows = pl.ds(into, rows_t, stride=tiles)
                    final[at_rows, :] = jnp.where(inside, turned, final[at_rows, :])

    done = pltpu.make_async_copy(final, out, out_sem.at[0])
    done.start()
    for copy in started:
        copy.wait_send()
    for e in range(1, chips):
        for i in range(q):
            for h in range(cuts):
                for j in range(tiles):
                    p_cross(e, i, h, j).wait_send()
    done.wait()


def per_device(n, n_aux, amplitudes, fitting):
    rows_t, pair_dev, width = amplitudes.shape
    count_fit, rows_b, _ = fitting.shape
    assert pair_dev == 1 and count_fit == 1 and rows_t % rows_b == 0
    chips = n_aux // 2
    parts = max([p for p in range(1, PARTS + 1) if rows_t % (16 * p) == 0], default=1)
    cuts = CUTS if rows_b % 16 == 0 and n > 2 else 1
    reach = n // 2
    lanes = 128
    tiles = width // lanes
    q = rows_t // rows_b
    dma = pltpu.SemaphoreType.DMA
    half = pltpu.VMEM((width, width), BF16)
    tiled = pltpu.VMEM((tiles, lanes, 2 * width), BF16)
    block = pltpu.VMEM((chips * q, rows_b, 2 * width), BF16)
    out = pl.pallas_call(
        functools.partial(kernel, n, chips, parts, cuts),
        out_shape=jax.ShapeDtypeStruct((rows_t * tiles, lanes), F32),
        in_specs=[pl.BlockSpec(memory_space=pltpu.HBM)] * 2,
        out_specs=pl.BlockSpec(memory_space=pl.ANY),
        scratch_shapes=[
            pltpu.VMEM((width * tiles, lanes), F32), half, half,
            pltpu.VMEM((2, width, width), F32), tiled, tiled, block, block,
            pltpu.VMEM((chips - 1, tiles, q * rows_b, lanes), F32),
            pltpu.VMEM((chips - 1, tiles, q * rows_b, lanes), F32),
            pltpu.VMEM((tiles, q * rows_b, lanes), F32), pltpu.VMEM((rows_t * tiles, lanes), F32),
            pltpu.VMEM((chips * q, 2 * rows_b, width), F32),
            dma((2,)), dma((1,)),
            dma((reach, cuts)), dma((reach, cuts)), dma((reach, cuts)), dma((reach, cuts)),
            dma((reach + 1, 2, cuts)), dma((reach + 1, 2, cuts)),
            dma((chips - 1, parts)), dma((chips - 1, parts)),
            dma((chips, parts)), dma((chips, parts)),
            dma((chips - 1, q, cuts, tiles)), dma((chips - 1, q, cuts, tiles)),
        ],
        compiler_params=pltpu.CompilerParams(
            collective_id=0, has_side_effects=True, vmem_limit_bytes=105 << 19
        ),
    )(*[pltpu.with_memory_space_constraint(v, pltpu.HBM) for v in (
        amplitudes.reshape(rows_t * tiles, lanes), fitting.reshape(rows_b, width))])
    return out.reshape(rows_t, pair_dev, width)


def solution(mesh):
    spec = P("aux", "pair", None)
    return jax.shard_map(
        functools.partial(per_device, mesh.shape["pair"], mesh.shape["aux"]),
        mesh=mesh, in_specs=(spec, spec), out_specs=spec, check_vma=False,
    )
```

```python
import functools

import jax
import jax.numpy as jnp
from jax import lax
from jax.experimental import pallas as pl
from jax.experimental.pallas import tpu as pltpu
from jax.sharding import PartitionSpec as P

MESH = pl.DeviceIdType.MESH
CUTS, PARTS = 2, 4
F32, BF16 = jnp.float32, jnp.bfloat16
NT = (((1,), (1,)), ((), ()))


def ring_order(n):
    depth = 4 if n % 4 == 0 and n > 4 else 2
    width = n // depth
    if n % 2 or width < 2:
        return list(range(n))
    walk = []
    for z in range(depth):
        ys = range(1, width) if z % 2 == 0 else range(width - 1, 0, -1)
        walk += [z * width + y for y in ys]
    return walk + [z * width for z in range(depth - 1, -1, -1)]


def lookup(table, key):
    return sum(jnp.where(key == k, v, 0) for k, v in enumerate(table))


def split(v):
    high = v.astype(BF16).astype(F32)
    return high, v - high


def kernel(
    n, chips, parts, cuts,
    t_in, b_in, out,
    t_all, t_high, t_low, b_all, b_high, b_low, g_high, g_low,
    outbox, inbox, mine, final, g_ahead,
    local_sem, out_sem, right_send, right_recv, left_send, left_recv, bm_send, bm_recv,
    tx_send, tx_recv, tm_send, tm_recv, px_send, px_recv,
):
    rows_b, width = b_in.shape
    lanes = t_in.shape[1]
    tiles = width // lanes
    rows_t = t_in.shape[0] // tiles
    piece = rows_t // parts
    q = rows_t // rows_b
    reach = n // 2
    order = ring_order(n)
    where = [order.index(k) for k in range(n)]
    pair, aux = lax.axis_index("pair"), lax.axis_index("aux")
    chip, core = aux // 2, aux % 2
    mate = chip * 2 + (1 - core)
    spot = lookup(where, pair)

    def at(step):
        return lookup(order, lax.rem(spot + step + n, n))

    right, left = at(1), at(-1)

    def chip_at(step):
        return lax.rem(chip + step + chips, chips)

    barrier = pltpu.get_barrier_semaphore()
    greet = [(right, aux), (left, aux), (pair, mate)]
    greet += [(pair, chip_at(e) * 2 + core) for e in range(1, chips)]
    for who in greet:
        pl.semaphore_signal(barrier, inc=1, device_id=who, device_id_type=MESH)
    pl.semaphore_wait(barrier, len(greet))

    sizes = [rows_b] if cuts == 1 else [(rows_b // 2 + 15) // 16 * 16, rows_b - (rows_b // 2 + 15) // 16 * 16]
    starts = [0, sizes[0]][:cuts]
    rounds = [(d, g) for d in range(1, reach) for g in range(cuts)] + [(reach, 0)]
    place, due, filled = {}, {}, [rows_b]
    for h in range(cuts):
        place[0, True, h] = place[0, False, h] = starts[h]
        due[0, True, h] = due[0, False, h] = 0

    def carried(d, from_left):
        return d < reach or cuts > 1 or from_left

    def cut_of(g, from_left):
        return g if from_left else cuts - 1 - g

    for v, (d, g) in enumerate(rounds, 1):
        count = filled[-1]
        for from_left in (True, False):
            if carried(d, from_left):
                h = cut_of(g, from_left)
                place[d, from_left, h], due[d, from_left, h] = count, v
                if d == reach:
                    place[d, not from_left, h], due[d, not from_left, h] = count, v
                count += sizes[h]
        filled.append(count)
    n_events = len(filled)
    first = min(cuts + 1, n_events - 1)
    for d in range(reach + 1):
        events = [due[d, side, h] for side in (True, False) for h in range(cuts)]
        if min(events) <= first < max(events):
            for side in (True, False):
                for h in range(cuts):
                    due[d, side, h] = max(events)

    def b_rows(d, from_left, h):
        return pl.ds(place[d, from_left, h], sizes[h])

    def t_rows(owner, s):
        start = (owner * rows_t + s * piece) * tiles
        return pl.ds(pl.multiple_of(start, 8), piece * tiles)

    def t_own(s):
        return pl.ds(s * piece * tiles, piece * tiles)

    def b_source(d, from_left, h):
        return b_in.at[pl.ds(starts[h], sizes[h])] if d == 0 else b_all.at[core, b_rows(d, from_left, h)]

    def hop(d, g, to_right):
        h = cut_of(g, to_right)
        send, recv = (right_send, right_recv) if to_right else (left_send, left_recv)
        return pltpu.make_async_remote_copy(
            src_ref=b_source(d - 1, to_right, h),
            dst_ref=b_all.at[core, b_rows(d, to_right, h)],
            send_sem=send.at[d - 1, h],
            recv_sem=recv.at[d - 1, h],
            device_id=(right if to_right else left, aux),
            device_id_type=MESH,
        )

    def arrive(d, g, from_left):
        h = cut_of(g, from_left)
        rows = b_rows(d, from_left, h)
        send, recv = (right_send, right_recv) if from_left else (left_send, left_recv)
        pltpu.make_async_remote_copy(
            src_ref=b_all.at[core, rows],
            dst_ref=b_all.at[core, rows],
            send_sem=send.at[d - 1, h],
            recv_sem=recv.at[d - 1, h],
            device_id=(left if from_left else right, aux),
            device_id_type=MESH,
        ).wait_recv()

    def b_mate(d, h, from_left, level):
        rows = b_rows(d, from_left, h)
        side = 0 if from_left else 1
        return pltpu.make_async_remote_copy(
            src_ref=b_source(d, from_left, h) if d == 0 else b_all.at[level, rows],
            dst_ref=b_all.at[level, rows],
            send_sem=bm_send.at[d, side, h],
            recv_sem=bm_recv.at[d, side, h],
            device_id=(pair, mate),
            device_id_type=MESH,
        )

    def t_cross(e, s):
        return pltpu.make_async_remote_copy(
            src_ref=t_in.at[t_own(s)],
            dst_ref=t_all.at[t_rows(aux, s)],
            send_sem=tx_send.at[e - 1, s],
            recv_sem=tx_recv.at[e - 1, s],
            device_id=(pair, chip_at(e) * 2 + core),
            device_id_type=MESH,
        )

    def t_mate(e, s):
        rows = t_rows(chip_at(-e) * 2 + core, s)
        return pltpu.make_async_remote_copy(
            src_ref=t_in.at[t_own(s)] if e == 0 else t_all.at[rows],
            dst_ref=t_all.at[rows],
            send_sem=tm_send.at[e, s],
            recv_sem=tm_recv.at[e, s],
            device_id=(pair, mate),
            device_id_type=MESH,
        )

    def t_landed(owner, s, send, recv):
        rows = t_rows(owner, s)
        pltpu.make_async_remote_copy(
            src_ref=t_all.at[rows], dst_ref=t_all.at[rows], send_sem=send, recv_sem=recv,
            device_id=(pair, mate), device_id_type=MESH,
        ).wait_recv()

    started = []

    def go(copy):
        copy.start()
        started.append(copy)

    for s in range(parts):
        for e in range(1, chips):
            go(t_cross(e, s))
        if s == 0:
            for g in range(cuts if reach > 1 else 1):
                for to_right in (True, False):
                    if carried(1, to_right):
                        go(hop(1, g, to_right))
    own_b = pltpu.make_async_copy(
        b_in, b_all.at[core, pl.ds(0, rows_b)], local_sem.at[0]
    )
    own_t = pltpu.make_async_copy(
        t_in, t_all.at[pl.ds(pl.multiple_of(aux * rows_t * tiles, 8), rows_t * tiles)], local_sem.at[1]
    )
    own_t.start()
    own_b.start()
    for s in range(parts):
        go(t_mate(0, s))
    for h in range(cuts):
        go(b_mate(0, h, True, core))

    aligned = piece % 16 == 0

    def t_split(start, size):
        rows = pl.ds(pl.multiple_of(start, 16), size)
        for k in range(tiles):
            high, low = split(t_all[pl.ds(start * tiles + k, size, stride=tiles), :])
            t_high[rows, k * lanes:(k + 1) * lanes] = high.astype(BF16)
            t_low[rows, k * lanes:(k + 1) * lanes] = low.astype(BF16)

    def t_part(owner, s):
        if aligned:
            t_split(owner * rows_t + s * piece, piece)

    def t_over(e, s):
        owner = chip_at(-e) * 2 + (1 - core)
        t_landed(owner, s, tm_send.at[e, s], tm_recv.at[e, s])
        t_part(owner, s)

    def relay(v):
        d, g = rounds[v - 1]
        for from_left in sorted((True, False), key=lambda side: sizes[cut_of(g, side)]):
            if carried(d, from_left):
                arrive(d, g, from_left)
                if d + 1 < reach or (d + 1 == reach and g == 0 and carried(reach, from_left)):
                    go(hop(d + 1, g, from_left))
                go(b_mate(d, cut_of(g, from_left), from_left, core))

    def b_over(v):
        if v == 0:
            for h in range(cuts):
                b_mate(0, h, True, 1 - core).wait_recv()
            return
        d, g = rounds[v - 1]
        for from_left in (True, False):
            if carried(d, from_left):
                b_mate(d, cut_of(g, from_left), from_left, 1 - core).wait_recv()

    def t_step(s):
        for e in range(1, chips):
            owner = chip_at(-e) * 2 + core
            t_landed(owner, s, tx_send.at[e - 1, s], tx_recv.at[e - 1, s])
            go(t_mate(e, s))
            t_part(owner, s)
        if s:
            for e in range(1, chips):
                t_over(e, s - 1)

    own_t.wait()
    if aligned:
        @pl.loop(0, parts)
        def _(s):
            t_part(aux, s)

        for s in range(parts):
            t_over(0, s)
    else:
        for s in range(parts):
            t_over(0, s)
    own_b.wait()

    def first_block(slot):
        return (chip_at(slot // q) * 2 + core) * q + lax.rem(slot, q)

    def reach_of(o):
        return (o, False) if o <= reach and o < n - o else (n - o, True)

    def about(table, slot, h):
        away = lax.rem(lookup(where, first_block(slot)) - spot + n, n)
        return lookup([table[reach_of(o) + (h,)] for o in range(n)], away)

    ready = [[about(due, slot, h) for h in range(cuts)] for slot in range(chips * q)]
    origin = [[about(place, slot, h) for h in range(cuts)] for slot in range(chips * q)]

    def pick(table, slot, h):
        return lookup([row[h] for row in table], slot)

    def extent(h):
        return (starts[h], sizes[h]) if h is not None else (0, rows_b)

    ahead = (2 * rows_t // lanes) if chips == 2 and aligned else 0
    near = pl.ds(pl.multiple_of(chip * (tiles - ahead) * lanes, lanes), ahead * lanes)
    rest_of = pl.ds(pl.multiple_of((1 - chip) * ahead * lanes, lanes), (tiles - ahead) * lanes)

    def g_sum(slot, h, span):
        count = extent(h)[1]
        cuts_in = range(cuts) if h is None else [h]
        pieces = []
        for level in range(2):
            parts_in = [
                b_all[level, pl.ds(pl.multiple_of(pick(origin, slot, c), 8), sizes[c]), span] for c in cuts_in
            ]
            pieces.append(split(jnp.concatenate(parts_in, axis=0) if len(parts_in) > 1 else parts_in[0]))
        high = jnp.concatenate([p[0] for p in pieces], axis=0)
        low = jnp.concatenate([p[1] for p in pieces], axis=0)
        both = jnp.concatenate([high, low], axis=0).astype(BF16)
        main = jnp.dot(both, t_high[span, :], preferred_element_type=F32)
        rest = jnp.dot(high.astype(BF16), t_low[span, :], preferred_element_type=F32)
        return main[:2 * count] + (main[2 * count:] + rest)

    def g_part(slot, h, begun_before=False):
        start, count = extent(h)
        if begun_before:
            total = g_ahead[slot] + g_sum(slot, h, rest_of)
        else:
            total = g_sum(slot, h, slice(None))
        high, low = split(total)
        for level in range(2):
            part = slice(level * count, (level + 1) * count)
            lane = slice(level * width, (level + 1) * width)
            g_high[slot, start:start + count, lane] = high[part].astype(BF16)
            g_low[slot, start:start + count, lane] = low[part].astype(BF16)

    def product(high, low, cols_high, cols_low):
        rows = high.shape[0]
        dot = functools.partial(lax.dot_general, dimension_numbers=NT, preferred_element_type=F32)
        if rows_b % 16 == 0:
            main = dot(jnp.concatenate([high, low], axis=0), cols_high)
            return main[:rows] + (main[rows:] + dot(high, cols_low))
        return dot(high, cols_high) + (dot(low, cols_high) + dot(high, cols_low))

    def columns(j, count):
        return [ref[pl.ds(j, count)].reshape(count * lanes, 2 * width) for ref in (b_high, b_low)]

    def p_cross(e, i, h, j):
        rows = pl.ds(pl.multiple_of(i * rows_b + starts[h], 8), sizes[h])
        return pltpu.make_async_remote_copy(
            src_ref=outbox.at[e - 1, j, rows], dst_ref=inbox.at[e - 1, j, rows],
            send_sem=px_send.at[e - 1, i, h, j], recv_sem=px_recv.at[e - 1, i, h, j],
            device_id=(pair, chip_at(e) * 2 + core), device_id_type=MESH,
        )

    def full(v):
        return filled[v] // lanes

    def older(v, j):
        @pl.loop(q, slots)
        def _(turn):
            slot = slot_of(turn - q)
            e, i = slot // q, lax.rem(slot, q)
            old = [pick(ready, slot, h) < v for h in range(cuts)]

            @pl.when(functools.reduce(jnp.logical_or, old))
            def _():
                rows = pl.ds(pl.multiple_of(i * rows_b, 8), rows_b)
                outbox[e - 1, j, rows] = product(g_high[slot], g_low[slot], *columns(j, 1))
                for h in range(cuts):
                    @pl.when(old[h])
                    def _(h=h):
                        p_cross(e, i, h, j).start()

    def block_ready(slot):
        return functools.reduce(jnp.maximum, [pick(ready, slot, h) for h in range(cuts)])

    slots = chips * q
    swaps = [jnp.where(block_ready(e * q + 1) < block_ready(e * q), 1, 0) if q == 2 else 0 for e in range(chips)]

    def slot_of(turn):
        if chips == 2 and q == 2:
            e = 1 - turn // 2
            return e * q + lax.rem(turn + lookup(swaps, e), 2)
        return lax.rem(turn + q, slots)

    def newer(h, count, wanted, low=0, high=slots, begun_before=False):
        start, size = extent(h)

        @pl.loop(low, high)
        def _(turn):
            slot = slot_of(turn)
            e, i = slot // q, lax.rem(slot, q)

            @pl.when(wanted(slot))
            def _():
                g_part(slot, h, begun_before)

                @pl.when(e > 0)
                def _():
                    rows = pl.ds(pl.multiple_of(i * rows_b + start, 8), size)
                    left = [ref[slot, start:start + size, :] for ref in (g_high, g_low)]

                    def some(j, k):
                        value = product(*left, *columns(j, k))
                        for t in range(k):
                            outbox[e - 1, j + t, rows] = value[:, t * lanes:(t + 1) * lanes]
                            for c in range(cuts) if h is None else [h]:
                                p_cross(e, i, c, j + t).start()

                    if count // 2:
                        @pl.loop(0, count // 2)
                        def _(k):
                            some(2 * k, 2)
                    if count % 2:
                        some(count - 1, 1)

    def tile_split(j):
        for level in range(2):
            high, low = split(b_all[level, pl.ds(j * lanes, lanes), :])
            b_high[j, :, level * width:(level + 1) * width] = high.astype(BF16)
            b_low[j, :, level * width:(level + 1) * width] = low.astype(BF16)

    def prepare(v):
        b_over(v)
        for j in range(full(v - 1) if v else 0, full(v)):
            tile_split(j)

    def begun(slot):
        return block_ready(slot) <= first

    assert all(v < first for (d, _, _), v in due.items() if v <= first) or not ahead
    prepare(0)
    step = 0
    for v in range(1, first + 1):
        upto = parts * (2 * v - 1) // (2 * first)
        for s in range(step, upto):
            t_step(s)
        step = upto
        relay(v)
        if v > 1:
            prepare(v - 1)
    if ahead:
        @pl.loop(0, slots)
        def _(turn):
            slot = slot_of(turn)

            @pl.when(begun(slot))
            def _():
                g_ahead[slot] = g_sum(slot, None, near)

    for s in range(step, parts):
        t_step(s)
    if first + 1 < n_events:
        relay(first + 1)
    for e in range(1, chips):
        t_over(e, parts - 1)
    if not aligned:
        @pl.loop(0, width // 128)
        def _(i):
            t_split(i * 128, 128)
    prepare(first)

    def own_columns(j, count):
        if rows_b % 16 == 0:
            left = [ref[:q].reshape(q * rows_b, 2 * width) for ref in (g_high, g_low)]
            value = product(*left, *columns(j, count))
            for k in range(count):
                mine[j + k] = value[:, k * lanes:(k + 1) * lanes]
        else:
            for k in range(count):
                @pl.loop(0, q)
                def _(i):
                    mine[j + k, pl.ds(pl.multiple_of(i * rows_b, 8), rows_b)] = product(
                        g_high[i], g_low[i], *columns(j + k, 1))

    def own_pairs(low, high):
        @pl.loop(low, high)
        def _(k):
            own_columns(2 * k, 2)

    base = min(first + 1, n_events - 1)
    if base > first:
        prepare(base)

    def joined(slot):
        return block_ready(slot) == base

    late = block_ready(slot_of(slots - q - 1)) > base

    def group(low, high, when=True):
        newer(None, full(base), lambda slot: jnp.logical_and(begun(slot), when), low, high, bool(ahead))
        if base > first:
            newer(None, full(base), lambda slot: jnp.logical_and(joined(slot), when), low, high)

    some = (slots - q + 1) // 2
    most = slots - q + q // 2
    idle = block_ready(slot_of(0)) > base
    group(0, some)
    group(slots - q, slots, idle)
    if first + 2 < n_events:
        relay(first + 2)
    group(some, slots - q)
    group(slots - q, most, jnp.logical_not(idle))
    group(most, slots, jnp.logical_and(late, jnp.logical_not(idle)))
    for v in range(base + 1, n_events):
        if v > first + 2:
            relay(v)
        prepare(v)
        for j in range(full(v - 1), full(v)):
            older(v, j)
        if cuts == 1 or v == n_events - 1:
            newer(None, full(v), lambda slot: block_ready(slot) == v)
        else:
            for h in range(cuts):
                newer(h, full(v), lambda slot: pick(ready, slot, h) == v)

    group(most, slots, jnp.logical_not(jnp.logical_or(idle, late)))
    own_pairs(0, tiles // 2)
    if tiles % 2:
        own_columns(tiles - 1, 1)

    def block_of(d, from_left):
        return at(-d if from_left else d)

    segments = [[] for _ in range(tiles)]
    seen = set()
    for (d, from_left, h), begin in sorted(place.items(), key=lambda item: item[1]):
        if begin in seen:
            continue
        seen.add(begin)
        for j in range(begin // lanes, (begin + sizes[h] - 1) // lanes + 1):
            low, high = max(begin, j * lanes), min(begin + sizes[h], (j + 1) * lanes)
            segments[j].append((low - j * lanes, high - low, d, from_left, starts[h] + low - begin))

    lane = lax.broadcasted_iota(jnp.int32, (1, lanes), 1)

    for j in range(tiles):
        for e in range(1, chips):
            for i in range(q):
                for h in range(cuts):
                    p_cross(e, i, h, j).wait_recv()
        total = mine[j]
        for e in range(1, chips):
            total = total + inbox[e - 1, j]
        for begin, size, d, from_left, offset in segments[j]:
            goal = block_of(d, from_left) * rows_b + offset
            turned = pltpu.roll(total, lax.rem(goal - begin + lanes, lanes), 1)
            for part in range(2):
                into = goal // lanes + part
                inside = jnp.logical_and(lane >= goal - into * lanes, lane < goal - into * lanes + size)

                @pl.when(goal + size > into * lanes)
                def _():
                    at_rows = pl.ds(into, rows_t, stride=tiles)
                    final[at_rows, :] = jnp.where(inside, turned, final[at_rows, :])

    done = pltpu.make_async_copy(final, out, out_sem.at[0])
    done.start()
    for copy in started:
        copy.wait_send()
    for e in range(1, chips):
        for i in range(q):
            for h in range(cuts):
                for j in range(tiles):
                    p_cross(e, i, h, j).wait_send()
    done.wait()


def per_device(n, n_aux, amplitudes, fitting):
    rows_t, pair_dev, width = amplitudes.shape
    count_fit, rows_b, _ = fitting.shape
    assert pair_dev == 1 and count_fit == 1 and rows_t % rows_b == 0
    chips = n_aux // 2
    parts = max([p for p in range(1, PARTS + 1) if rows_t % (16 * p) == 0], default=1)
    cuts = CUTS if rows_b % 16 == 0 and n > 2 else 1
    reach = n // 2
    lanes = 128
    tiles = width // lanes
    q = rows_t // rows_b
    dma = pltpu.SemaphoreType.DMA
    half = pltpu.VMEM((width, width), BF16)
    tiled = pltpu.VMEM((tiles, lanes, 2 * width), BF16)
    block = pltpu.VMEM((chips * q, rows_b, 2 * width), BF16)
    out = pl.pallas_call(
        functools.partial(kernel, n, chips, parts, cuts),
        out_shape=jax.ShapeDtypeStruct((rows_t * tiles, lanes), F32),
        in_specs=[pl.BlockSpec(memory_space=pltpu.HBM)] * 2,
        out_specs=pl.BlockSpec(memory_space=pl.ANY),
        scratch_shapes=[
            pltpu.VMEM((width * tiles, lanes), F32), half, half,
            pltpu.VMEM((2, width, width), F32), tiled, tiled, block, block,
            pltpu.VMEM((chips - 1, tiles, q * rows_b, lanes), F32),
            pltpu.VMEM((chips - 1, tiles, q * rows_b, lanes), F32),
            pltpu.VMEM((tiles, q * rows_b, lanes), F32), pltpu.VMEM((rows_t * tiles, lanes), F32),
            pltpu.VMEM((chips * q, 2 * rows_b, width), F32),
            dma((2,)), dma((1,)),
            dma((reach, cuts)), dma((reach, cuts)), dma((reach, cuts)), dma((reach, cuts)),
            dma((reach + 1, 2, cuts)), dma((reach + 1, 2, cuts)),
            dma((chips - 1, parts)), dma((chips - 1, parts)),
            dma((chips, parts)), dma((chips, parts)),
            dma((chips - 1, q, cuts, tiles)), dma((chips - 1, q, cuts, tiles)),
        ],
        compiler_params=pltpu.CompilerParams(
            collective_id=0, has_side_effects=True, vmem_limit_bytes=105 << 19
        ),
    )(*[pltpu.with_memory_space_constraint(v, pltpu.HBM) for v in (
        amplitudes.reshape(rows_t * tiles, lanes), fitting.reshape(rows_b, width))])
    return out.reshape(rows_t, pair_dev, width)


def solution(mesh):
    spec = P("aux", "pair", None)
    return jax.shard_map(
        functools.partial(per_device, mesh.shape["pair"], mesh.shape["aux"]),
        mesh=mesh, in_specs=(spec, spec), out_specs=spec, check_vma=False,
    )
```

```python
import functools

import jax
import jax.numpy as jnp
from jax import lax
from jax.experimental import pallas as pl
from jax.experimental.pallas import tpu as pltpu
from jax.sharding import PartitionSpec as P

MESH = pl.DeviceIdType.MESH
CUTS, PARTS = 2, 4
F32, BF16 = jnp.float32, jnp.bfloat16
NT = (((1,), (1,)), ((), ()))


def ring_order(n):
    depth = 4 if n % 4 == 0 and n > 4 else 2
    width = n // depth
    if n % 2 or width < 2:
        return list(range(n))
    walk = []
    for z in range(depth):
        ys = range(1, width) if z % 2 == 0 else range(width - 1, 0, -1)
        walk += [z * width + y for y in ys]
    return walk + [z * width for z in range(depth - 1, -1, -1)]


def lookup(table, key):
    return sum(jnp.where(key == k, v, 0) for k, v in enumerate(table))


def split(v):
    high = v.astype(BF16).astype(F32)
    return high, v - high


def kernel(
    n, chips, parts, cuts,
    t_in, b_in, out,
    t_all, t_high, t_low, b_all, b_high, b_low, g_high, g_low,
    outbox, inbox, mine, final, g_ahead,
    local_sem, out_sem, right_send, right_recv, left_send, left_recv, bm_send, bm_recv,
    tx_send, tx_recv, tm_send, tm_recv, px_send, px_recv,
):
    rows_b, width = b_in.shape
    lanes = t_in.shape[1]
    tiles = width // lanes
    rows_t = t_in.shape[0] // tiles
    piece = rows_t // parts
    q = rows_t // rows_b
    reach = n // 2
    order = ring_order(n)
    where = [order.index(k) for k in range(n)]
    pair, aux = lax.axis_index("pair"), lax.axis_index("aux")
    chip, core = aux // 2, aux % 2
    mate = chip * 2 + (1 - core)
    spot = lookup(where, pair)

    def at(step):
        return lookup(order, lax.rem(spot + step + n, n))

    right, left = at(1), at(-1)

    def chip_at(step):
        return lax.rem(chip + step + chips, chips)

    barrier = pltpu.get_barrier_semaphore()
    greet = [(right, aux), (left, aux), (pair, mate)]
    greet += [(pair, chip_at(e) * 2 + core) for e in range(1, chips)]
    for who in greet:
        pl.semaphore_signal(barrier, inc=1, device_id=who, device_id_type=MESH)
    pl.semaphore_wait(barrier, len(greet))

    sizes = [rows_b] if cuts == 1 else [(rows_b // 2 + 15) // 16 * 16, rows_b - (rows_b // 2 + 15) // 16 * 16]
    starts = [0, sizes[0]][:cuts]
    rounds = [(d, g) for d in range(1, reach) for g in range(cuts)] + [(reach, 0)]
    place, due, filled = {}, {}, [rows_b]
    for h in range(cuts):
        place[0, True, h] = place[0, False, h] = starts[h]
        due[0, True, h] = due[0, False, h] = 0

    def carried(d, from_left):
        return d < reach or cuts > 1 or from_left

    def cut_of(g, from_left):
        return g if from_left else cuts - 1 - g

    for v, (d, g) in enumerate(rounds, 1):
        count = filled[-1]
        for from_left in (True, False):
            if carried(d, from_left):
                h = cut_of(g, from_left)
                place[d, from_left, h], due[d, from_left, h] = count, v
                if d == reach:
                    place[d, not from_left, h], due[d, not from_left, h] = count, v
                count += sizes[h]
        filled.append(count)
    n_events = len(filled)
    first = min(cuts + 1, n_events - 1)
    for d in range(reach + 1):
        events = [due[d, side, h] for side in (True, False) for h in range(cuts)]
        if min(events) <= first < max(events):
            for side in (True, False):
                for h in range(cuts):
                    due[d, side, h] = max(events)

    def b_rows(d, from_left, h):
        return pl.ds(place[d, from_left, h], sizes[h])

    def t_rows(owner, s):
        start = (owner * rows_t + s * piece) * tiles
        return pl.ds(pl.multiple_of(start, 8), piece * tiles)

    def t_own(s):
        return pl.ds(s * piece * tiles, piece * tiles)

    def b_source(d, from_left, h):
        return b_in.at[pl.ds(starts[h], sizes[h])] if d == 0 else b_all.at[core, b_rows(d, from_left, h)]

    def hop(d, g, to_right):
        h = cut_of(g, to_right)
        send, recv = (right_send, right_recv) if to_right else (left_send, left_recv)
        return pltpu.make_async_remote_copy(
            src_ref=b_source(d - 1, to_right, h),
            dst_ref=b_all.at[core, b_rows(d, to_right, h)],
            send_sem=send.at[d - 1, h],
            recv_sem=recv.at[d - 1, h],
            device_id=(right if to_right else left, aux),
            device_id_type=MESH,
        )

    def arrive(d, g, from_left):
        h = cut_of(g, from_left)
        rows = b_rows(d, from_left, h)
        send, recv = (right_send, right_recv) if from_left else (left_send, left_recv)
        pltpu.make_async_remote_copy(
            src_ref=b_all.at[core, rows],
            dst_ref=b_all.at[core, rows],
            send_sem=send.at[d - 1, h],
            recv_sem=recv.at[d - 1, h],
            device_id=(left if from_left else right, aux),
            device_id_type=MESH,
        ).wait_recv()

    def b_mate(d, h, from_left, level):
        rows = b_rows(d, from_left, h)
        side = 0 if from_left else 1
        return pltpu.make_async_remote_copy(
            src_ref=b_source(d, from_left, h) if d == 0 else b_all.at[level, rows],
            dst_ref=b_all.at[level, rows],
            send_sem=bm_send.at[d, side, h],
            recv_sem=bm_recv.at[d, side, h],
            device_id=(pair, mate),
            device_id_type=MESH,
        )

    def t_cross(e, s):
        return pltpu.make_async_remote_copy(
            src_ref=t_in.at[t_own(s)],
            dst_ref=t_all.at[t_rows(aux, s)],
            send_sem=tx_send.at[e - 1, s],
            recv_sem=tx_recv.at[e - 1, s],
            device_id=(pair, chip_at(e) * 2 + core),
            device_id_type=MESH,
        )

    def t_mate(e, s):
        rows = t_rows(chip_at(-e) * 2 + core, s)
        return pltpu.make_async_remote_copy(
            src_ref=t_in.at[t_own(s)] if e == 0 else t_all.at[rows],
            dst_ref=t_all.at[rows],
            send_sem=tm_send.at[e, s],
            recv_sem=tm_recv.at[e, s],
            device_id=(pair, mate),
            device_id_type=MESH,
        )

    def t_landed(owner, s, send, recv):
        rows = t_rows(owner, s)
        pltpu.make_async_remote_copy(
            src_ref=t_all.at[rows], dst_ref=t_all.at[rows], send_sem=send, recv_sem=recv,
            device_id=(pair, mate), device_id_type=MESH,
        ).wait_recv()

    started = []

    def go(copy):
        copy.start()
        started.append(copy)

    for s in range(parts):
        for e in range(1, chips):
            go(t_cross(e, s))
        if s == 0:
            for g in range(cuts if reach > 1 else 1):
                for to_right in (True, False):
                    if carried(1, to_right):
                        go(hop(1, g, to_right))
    own_b = pltpu.make_async_copy(
        b_in, b_all.at[core, pl.ds(0, rows_b)], local_sem.at[0]
    )
    own_t = pltpu.make_async_copy(
        t_in, t_all.at[pl.ds(pl.multiple_of(aux * rows_t * tiles, 8), rows_t * tiles)], local_sem.at[1]
    )
    own_t.start()
    own_b.start()
    for s in range(parts):
        go(t_mate(0, s))
    for h in range(cuts):
        go(b_mate(0, h, True, core))

    aligned = piece % 16 == 0

    def t_split(start, size):
        rows = pl.ds(pl.multiple_of(start, 16), size)
        for k in range(tiles):
            high, low = split(t_all[pl.ds(start * tiles + k, size, stride=tiles), :])
            t_high[rows, k * lanes:(k + 1) * lanes] = high.astype(BF16)
            t_low[rows, k * lanes:(k + 1) * lanes] = low.astype(BF16)

    def t_part(owner, s):
        if aligned:
            t_split(owner * rows_t + s * piece, piece)

    def t_over(e, s):
        owner = chip_at(-e) * 2 + (1 - core)
        t_landed(owner, s, tm_send.at[e, s], tm_recv.at[e, s])
        t_part(owner, s)

    def relay(v):
        d, g = rounds[v - 1]
        for from_left in sorted((True, False), key=lambda side: sizes[cut_of(g, side)]):
            if carried(d, from_left):
                arrive(d, g, from_left)
                if d + 1 < reach or (d + 1 == reach and g == 0 and carried(reach, from_left)):
                    go(hop(d + 1, g, from_left))
                go(b_mate(d, cut_of(g, from_left), from_left, core))

    def b_over(v):
        if v == 0:
            for h in range(cuts):
                b_mate(0, h, True, 1 - core).wait_recv()
            return
        d, g = rounds[v - 1]
        for from_left in (True, False):
            if carried(d, from_left):
                b_mate(d, cut_of(g, from_left), from_left, 1 - core).wait_recv()

    def t_step(s):
        for e in range(1, chips):
            owner = chip_at(-e) * 2 + core
            t_landed(owner, s, tx_send.at[e - 1, s], tx_recv.at[e - 1, s])
            go(t_mate(e, s))
            t_part(owner, s)
        if s:
            for e in range(1, chips):
                t_over(e, s - 1)

    own_t.wait()
    if aligned:
        @pl.loop(0, parts)
        def _(s):
            t_part(aux, s)

        for s in range(parts):
            t_over(0, s)
    else:
        for s in range(parts):
            t_over(0, s)
    own_b.wait()

    def first_block(slot):
        return (chip_at(slot // q) * 2 + core) * q + lax.rem(slot, q)

    def reach_of(o):
        return (o, False) if o <= reach and o < n - o else (n - o, True)

    def about(table, slot, h):
        away = lax.rem(lookup(where, first_block(slot)) - spot + n, n)
        return lookup([table[reach_of(o) + (h,)] for o in range(n)], away)

    ready = [[about(due, slot, h) for h in range(cuts)] for slot in range(chips * q)]
    origin = [[about(place, slot, h) for h in range(cuts)] for slot in range(chips * q)]

    def pick(table, slot, h):
        return lookup([row[h] for row in table], slot)

    def extent(h):
        return (starts[h], sizes[h]) if h is not None else (0, rows_b)

    ahead = (2 * rows_t // lanes) if chips == 2 and aligned else 0
    near = pl.ds(pl.multiple_of(chip * (tiles - ahead) * lanes, lanes), ahead * lanes)
    rest_of = pl.ds(pl.multiple_of((1 - chip) * ahead * lanes, lanes), (tiles - ahead) * lanes)

    def g_sum(slot, h, span):
        count = extent(h)[1]
        cuts_in = range(cuts) if h is None else [h]
        pieces = []
        for level in range(2):
            parts_in = [
                b_all[level, pl.ds(pl.multiple_of(pick(origin, slot, c), 8), sizes[c]), span] for c in cuts_in
            ]
            pieces.append(split(jnp.concatenate(parts_in, axis=0) if len(parts_in) > 1 else parts_in[0]))
        high = jnp.concatenate([p[0] for p in pieces], axis=0)
        low = jnp.concatenate([p[1] for p in pieces], axis=0)
        both = jnp.concatenate([high, low], axis=0).astype(BF16)
        main = jnp.dot(both, t_high[span, :], preferred_element_type=F32)
        rest = jnp.dot(high.astype(BF16), t_low[span, :], preferred_element_type=F32)
        return main[:2 * count] + (main[2 * count:] + rest)

    def g_part(slot, h, begun_before=False):
        start, count = extent(h)
        if begun_before:
            total = g_ahead[slot] + g_sum(slot, h, rest_of)
        else:
            total = g_sum(slot, h, slice(None))
        high, low = split(total)
        for level in range(2):
            part = slice(level * count, (level + 1) * count)
            lane = slice(level * width, (level + 1) * width)
            g_high[slot, start:start + count, lane] = high[part].astype(BF16)
            g_low[slot, start:start + count, lane] = low[part].astype(BF16)

    def product(high, low, cols_high, cols_low):
        rows = high.shape[0]
        dot = functools.partial(lax.dot_general, dimension_numbers=NT, preferred_element_type=F32)
        if rows_b % 16 == 0:
            main = dot(jnp.concatenate([high, low], axis=0), cols_high)
            return main[:rows] + (main[rows:] + dot(high, cols_low))
        return dot(high, cols_high) + (dot(low, cols_high) + dot(high, cols_low))

    def columns(j, count):
        return [ref[pl.ds(j, count)].reshape(count * lanes, 2 * width) for ref in (b_high, b_low)]

    def p_cross(e, i, h, j):
        rows = pl.ds(pl.multiple_of(i * rows_b + starts[h], 8), sizes[h])
        return pltpu.make_async_remote_copy(
            src_ref=outbox.at[e - 1, j, rows], dst_ref=inbox.at[e - 1, j, rows],
            send_sem=px_send.at[e - 1, i, h, j], recv_sem=px_recv.at[e - 1, i, h, j],
            device_id=(pair, chip_at(e) * 2 + core), device_id_type=MESH,
        )

    def full(v):
        return filled[v] // lanes

    def older(v, j):
        @pl.loop(q, slots)
        def _(turn):
            slot = slot_of(turn - q)
            e, i = slot // q, lax.rem(slot, q)
            old = [pick(ready, slot, h) < v for h in range(cuts)]

            @pl.when(functools.reduce(jnp.logical_or, old))
            def _():
                rows = pl.ds(pl.multiple_of(i * rows_b, 8), rows_b)
                outbox[e - 1, j, rows] = product(g_high[slot], g_low[slot], *columns(j, 1))
                for h in range(cuts):
                    @pl.when(old[h])
                    def _(h=h):
                        p_cross(e, i, h, j).start()

    def block_ready(slot):
        return functools.reduce(jnp.maximum, [pick(ready, slot, h) for h in range(cuts)])

    slots = chips * q
    swaps = [jnp.where(block_ready(e * q + 1) < block_ready(e * q), 1, 0) if q == 2 else 0 for e in range(chips)]

    def slot_of(turn):
        if chips == 2 and q == 2:
            e = 1 - turn // 2
            return e * q + lax.rem(turn + lookup(swaps, e), 2)
        return lax.rem(turn + q, slots)

    def newer(h, count, wanted, low=0, high=slots, begun_before=False):
        start, size = extent(h)

        @pl.loop(low, high)
        def _(turn):
            slot = slot_of(turn)
            e, i = slot // q, lax.rem(slot, q)

            @pl.when(wanted(slot))
            def _():
                g_part(slot, h, begun_before)

                @pl.when(e > 0)
                def _():
                    rows = pl.ds(pl.multiple_of(i * rows_b + start, 8), size)
                    left = [ref[slot, start:start + size, :] for ref in (g_high, g_low)]

                    def some(j, k):
                        value = product(*left, *columns(j, k))
                        for t in range(k):
                            outbox[e - 1, j + t, rows] = value[:, t * lanes:(t + 1) * lanes]
                            for c in range(cuts) if h is None else [h]:
                                p_cross(e, i, c, j + t).start()

                    if count // 2:
                        @pl.loop(0, count // 2)
                        def _(k):
                            some(2 * k, 2)
                    if count % 2:
                        some(count - 1, 1)

    def tile_split(j):
        for level in range(2):
            high, low = split(b_all[level, pl.ds(j * lanes, lanes), :])
            b_high[j, :, level * width:(level + 1) * width] = high.astype(BF16)
            b_low[j, :, level * width:(level + 1) * width] = low.astype(BF16)

    def prepare(v):
        b_over(v)
        for j in range(full(v - 1) if v else 0, full(v)):
            tile_split(j)

    def begun(slot):
        return block_ready(slot) <= first

    assert all(v < first for (d, _, _), v in due.items() if v <= first) or not ahead
    def stage(wanted):
        if ahead:
            @pl.loop(0, slots)
            def _(turn):
                slot = slot_of(turn)

                @pl.when(wanted(slot))
                def _():
                    g_ahead[slot] = g_sum(slot, None, near)

    prepare(0)
    stage(lambda slot: block_ready(slot) == 0)
    step = 0
    for v in range(1, first + 1):
        upto = parts * (2 * v - 1) // (2 * first)
        for s in range(step, upto):
            t_step(s)
        step = upto
        relay(v)
        if v > 1:
            prepare(v - 1)
    stage(lambda slot: jnp.logical_and(begun(slot), block_ready(slot) > 0))
    prepare(first)
    for s in range(step, parts):
        t_step(s)
    if first + 1 < n_events:
        relay(first + 1)
    for e in range(1, chips):
        t_over(e, parts - 1)
    if not aligned:
        @pl.loop(0, width // 128)
        def _(i):
            t_split(i * 128, 128)

    def own_columns(j, count):
        if rows_b % 16 == 0:
            left = [ref[:q].reshape(q * rows_b, 2 * width) for ref in (g_high, g_low)]
            value = product(*left, *columns(j, count))
            for k in range(count):
                mine[j + k] = value[:, k * lanes:(k + 1) * lanes]
        else:
            for k in range(count):
                @pl.loop(0, q)
                def _(i):
                    mine[j + k, pl.ds(pl.multiple_of(i * rows_b, 8), rows_b)] = product(
                        g_high[i], g_low[i], *columns(j + k, 1))

    def own_pairs(low, high):
        @pl.loop(low, high)
        def _(k):
            own_columns(2 * k, 2)

    base = min(first + 1, n_events - 1)
    if base > first:
        prepare(base)

    def joined(slot):
        return block_ready(slot) == base

    late = block_ready(slot_of(slots - q - 1)) > base

    def group(low, high, when=True):
        newer(None, full(base), lambda slot: jnp.logical_and(begun(slot), when), low, high, bool(ahead))
        if base > first:
            newer(None, full(base), lambda slot: jnp.logical_and(joined(slot), when), low, high)

    some = (slots - q + 1) // 2
    most = slots - q + q // 2
    idle = block_ready(slot_of(0)) > base
    group(0, some)
    group(slots - q, slots, idle)
    if first + 2 < n_events:
        relay(first + 2)
    group(some, slots - q)
    group(slots - q, most, jnp.logical_not(idle))
    group(most, slots, jnp.logical_and(late, jnp.logical_not(idle)))
    for v in range(base + 1, n_events):
        if v > first + 2:
            relay(v)
        prepare(v)
        for j in range(full(v - 1), full(v)):
            older(v, j)
        if cuts == 1 or v == n_events - 1:
            newer(None, full(v), lambda slot: block_ready(slot) == v)
        else:
            for h in range(cuts):
                newer(h, full(v), lambda slot: pick(ready, slot, h) == v)

    group(most, slots, jnp.logical_not(jnp.logical_or(idle, late)))
    own_pairs(0, tiles // 2)
    if tiles % 2:
        own_columns(tiles - 1, 1)

    def block_of(d, from_left):
        return at(-d if from_left else d)

    segments = [[] for _ in range(tiles)]
    seen = set()
    for (d, from_left, h), begin in sorted(place.items(), key=lambda item: item[1]):
        if begin in seen:
            continue
        seen.add(begin)
        for j in range(begin // lanes, (begin + sizes[h] - 1) // lanes + 1):
            low, high = max(begin, j * lanes), min(begin + sizes[h], (j + 1) * lanes)
            segments[j].append((low - j * lanes, high - low, d, from_left, starts[h] + low - begin))

    lane = lax.broadcasted_iota(jnp.int32, (1, lanes), 1)

    for j in range(tiles):
        for e in range(1, chips):
            for i in range(q):
                for h in range(cuts):
                    p_cross(e, i, h, j).wait_recv()
        total = mine[j]
        for e in range(1, chips):
            total = total + inbox[e - 1, j]
        for begin, size, d, from_left, offset in segments[j]:
            goal = block_of(d, from_left) * rows_b + offset
            turned = pltpu.roll(total, lax.rem(goal - begin + lanes, lanes), 1)
            for part in range(2):
                into = goal // lanes + part
                inside = jnp.logical_and(lane >= goal - into * lanes, lane < goal - into * lanes + size)

                @pl.when(goal + size > into * lanes)
                def _():
                    at_rows = pl.ds(into, rows_t, stride=tiles)
                    final[at_rows, :] = jnp.where(inside, turned, final[at_rows, :])

    done = pltpu.make_async_copy(final, out, out_sem.at[0])
    done.start()
    for copy in started:
        copy.wait_send()
    for e in range(1, chips):
        for i in range(q):
            for h in range(cuts):
                for j in range(tiles):
                    p_cross(e, i, h, j).wait_send()
    done.wait()


def per_device(n, n_aux, amplitudes, fitting):
    rows_t, pair_dev, width = amplitudes.shape
    count_fit, rows_b, _ = fitting.shape
    assert pair_dev == 1 and count_fit == 1 and rows_t % rows_b == 0
    chips = n_aux // 2
    parts = max([p for p in range(1, PARTS + 1) if rows_t % (16 * p) == 0], default=1)
    cuts = CUTS if rows_b % 16 == 0 and n > 2 else 1
    reach = n // 2
    lanes = 128
    tiles = width // lanes
    q = rows_t // rows_b
    dma = pltpu.SemaphoreType.DMA
    half = pltpu.VMEM((width, width), BF16)
    tiled = pltpu.VMEM((tiles, lanes, 2 * width), BF16)
    block = pltpu.VMEM((chips * q, rows_b, 2 * width), BF16)
    out = pl.pallas_call(
        functools.partial(kernel, n, chips, parts, cuts),
        out_shape=jax.ShapeDtypeStruct((rows_t * tiles, lanes), F32),
        in_specs=[pl.BlockSpec(memory_space=pltpu.HBM)] * 2,
        out_specs=pl.BlockSpec(memory_space=pl.ANY),
        scratch_shapes=[
            pltpu.VMEM((width * tiles, lanes), F32), half, half,
            pltpu.VMEM((2, width, width), F32), tiled, tiled, block, block,
            pltpu.VMEM((chips - 1, tiles, q * rows_b, lanes), F32),
            pltpu.VMEM((chips - 1, tiles, q * rows_b, lanes), F32),
            pltpu.VMEM((tiles, q * rows_b, lanes), F32), pltpu.VMEM((rows_t * tiles, lanes), F32),
            pltpu.VMEM((chips * q, 2 * rows_b, width), F32),
            dma((2,)), dma((1,)),
            dma((reach, cuts)), dma((reach, cuts)), dma((reach, cuts)), dma((reach, cuts)),
            dma((reach + 1, 2, cuts)), dma((reach + 1, 2, cuts)),
            dma((chips - 1, parts)), dma((chips - 1, parts)),
            dma((chips, parts)), dma((chips, parts)),
            dma((chips - 1, q, cuts, tiles)), dma((chips - 1, q, cuts, tiles)),
        ],
        compiler_params=pltpu.CompilerParams(
            collective_id=0, has_side_effects=True, vmem_limit_bytes=105 << 19
        ),
    )(*[pltpu.with_memory_space_constraint(v, pltpu.HBM) for v in (
        amplitudes.reshape(rows_t * tiles, lanes), fitting.reshape(rows_b, width))])
    return out.reshape(rows_t, pair_dev, width)


def solution(mesh):
    spec = P("aux", "pair", None)
    return jax.shard_map(
        functools.partial(per_device, mesh.shape["pair"], mesh.shape["aux"]),
        mesh=mesh, in_specs=(spec, spec), out_specs=spec, check_vma=False,
    )
```

```python
import functools

import jax
import jax.numpy as jnp
from jax import lax
from jax.experimental import pallas as pl
from jax.experimental.pallas import tpu as pltpu
from jax.sharding import PartitionSpec as P

MESH = pl.DeviceIdType.MESH
CUTS, PARTS = 2, 4
F32, BF16 = jnp.float32, jnp.bfloat16
NT = (((1,), (1,)), ((), ()))


def ring_order(n):
    depth = 4 if n % 4 == 0 and n > 4 else 2
    width = n // depth
    if n % 2 or width < 2:
        return list(range(n))
    walk = []
    for z in range(depth):
        ys = range(1, width) if z % 2 == 0 else range(width - 1, 0, -1)
        walk += [z * width + y for y in ys]
    return walk + [z * width for z in range(depth - 1, -1, -1)]


def lookup(table, key):
    return sum(jnp.where(key == k, v, 0) for k, v in enumerate(table))


def split(v):
    high = v.astype(BF16).astype(F32)
    return high, v - high


def kernel(
    n, chips, parts, cuts,
    t_in, b_in, out,
    t_all, t_high, t_low, b_all, b_high, b_low, g_high, g_low,
    outbox, inbox, mine, final, g_ahead,
    local_sem, out_sem, right_send, right_recv, left_send, left_recv, bm_send, bm_recv,
    tx_send, tx_recv, tm_send, tm_recv, px_send, px_recv,
):
    rows_b, width = b_in.shape
    lanes = t_in.shape[1]
    tiles = width // lanes
    rows_t = t_in.shape[0] // tiles
    piece = rows_t // parts
    q = rows_t // rows_b
    reach = n // 2
    order = ring_order(n)
    where = [order.index(k) for k in range(n)]
    pair, aux = lax.axis_index("pair"), lax.axis_index("aux")
    chip, core = aux // 2, aux % 2
    mate = chip * 2 + (1 - core)
    spot = lookup(where, pair)

    def at(step):
        return lookup(order, lax.rem(spot + step + n, n))

    right, left = at(1), at(-1)

    def chip_at(step):
        return lax.rem(chip + step + chips, chips)

    barrier = pltpu.get_barrier_semaphore()
    greet = [(right, aux), (left, aux), (pair, mate)]
    greet += [(pair, chip_at(e) * 2 + core) for e in range(1, chips)]
    for who in greet:
        pl.semaphore_signal(barrier, inc=1, device_id=who, device_id_type=MESH)
    pl.semaphore_wait(barrier, len(greet))

    sizes = [rows_b] if cuts == 1 else [(rows_b // 2 + 15) // 16 * 16, rows_b - (rows_b // 2 + 15) // 16 * 16]
    starts = [0, sizes[0]][:cuts]
    rounds = [(d, g) for d in range(1, reach) for g in range(cuts)] + [(reach, 0)]
    place, due, filled = {}, {}, [rows_b]
    for h in range(cuts):
        place[0, True, h] = place[0, False, h] = starts[h]
        due[0, True, h] = due[0, False, h] = 0

    def carried(d, from_left):
        return d < reach or cuts > 1 or from_left

    def cut_of(g, from_left):
        return g if from_left else cuts - 1 - g

    for v, (d, g) in enumerate(rounds, 1):
        count = filled[-1]
        for from_left in (True, False):
            if carried(d, from_left):
                h = cut_of(g, from_left)
                place[d, from_left, h], due[d, from_left, h] = count, v
                if d == reach:
                    place[d, not from_left, h], due[d, not from_left, h] = count, v
                count += sizes[h]
        filled.append(count)
    n_events = len(filled)
    first = min(cuts + 1, n_events - 1)
    for d in range(reach + 1):
        events = [due[d, side, h] for side in (True, False) for h in range(cuts)]
        if min(events) <= first < max(events):
            for side in (True, False):
                for h in range(cuts):
                    due[d, side, h] = max(events)

    def b_rows(d, from_left, h):
        return pl.ds(place[d, from_left, h], sizes[h])

    def t_rows(owner, s):
        start = (owner * rows_t + s * piece) * tiles
        return pl.ds(pl.multiple_of(start, 8), piece * tiles)

    def t_own(s):
        return pl.ds(s * piece * tiles, piece * tiles)

    def b_source(d, from_left, h):
        return b_in.at[pl.ds(starts[h], sizes[h])] if d == 0 else b_all.at[core, b_rows(d, from_left, h)]

    def hop(d, g, to_right):
        h = cut_of(g, to_right)
        send, recv = (right_send, right_recv) if to_right else (left_send, left_recv)
        return pltpu.make_async_remote_copy(
            src_ref=b_source(d - 1, to_right, h),
            dst_ref=b_all.at[core, b_rows(d, to_right, h)],
            send_sem=send.at[d - 1, h],
            recv_sem=recv.at[d - 1, h],
            device_id=(right if to_right else left, aux),
            device_id_type=MESH,
        )

    def arrive(d, g, from_left):
        h = cut_of(g, from_left)
        rows = b_rows(d, from_left, h)
        send, recv = (right_send, right_recv) if from_left else (left_send, left_recv)
        pltpu.make_async_remote_copy(
            src_ref=b_all.at[core, rows],
            dst_ref=b_all.at[core, rows],
            send_sem=send.at[d - 1, h],
            recv_sem=recv.at[d - 1, h],
            device_id=(left if from_left else right, aux),
            device_id_type=MESH,
        ).wait_recv()

    def b_mate(d, h, from_left, level):
        rows = b_rows(d, from_left, h)
        side = 0 if from_left else 1
        return pltpu.make_async_remote_copy(
            src_ref=b_source(d, from_left, h) if d == 0 else b_all.at[level, rows],
            dst_ref=b_all.at[level, rows],
            send_sem=bm_send.at[d, side, h],
            recv_sem=bm_recv.at[d, side, h],
            device_id=(pair, mate),
            device_id_type=MESH,
        )

    def t_cross(e, s):
        return pltpu.make_async_remote_copy(
            src_ref=t_in.at[t_own(s)],
            dst_ref=t_all.at[t_rows(aux, s)],
            send_sem=tx_send.at[e - 1, s],
            recv_sem=tx_recv.at[e - 1, s],
            device_id=(pair, chip_at(e) * 2 + core),
            device_id_type=MESH,
        )

    def t_mate(e, s):
        rows = t_rows(chip_at(-e) * 2 + core, s)
        return pltpu.make_async_remote_copy(
            src_ref=t_in.at[t_own(s)] if e == 0 else t_all.at[rows],
            dst_ref=t_all.at[rows],
            send_sem=tm_send.at[e, s],
            recv_sem=tm_recv.at[e, s],
            device_id=(pair, mate),
            device_id_type=MESH,
        )

    def t_landed(owner, s, send, recv):
        rows = t_rows(owner, s)
        pltpu.make_async_remote_copy(
            src_ref=t_all.at[rows], dst_ref=t_all.at[rows], send_sem=send, recv_sem=recv,
            device_id=(pair, mate), device_id_type=MESH,
        ).wait_recv()

    started = []

    def go(copy):
        copy.start()
        started.append(copy)

    for s in range(parts):
        for e in range(1, chips):
            go(t_cross(e, s))
        if s == 0:
            for g in range(cuts if reach > 1 else 1):
                for to_right in (True, False):
                    if carried(1, to_right):
                        go(hop(1, g, to_right))
    own_b = pltpu.make_async_copy(
        b_in, b_all.at[core, pl.ds(0, rows_b)], local_sem.at[0]
    )
    own_t = pltpu.make_async_copy(
        t_in, t_all.at[pl.ds(pl.multiple_of(aux * rows_t * tiles, 8), rows_t * tiles)], local_sem.at[1]
    )
    own_t.start()
    own_b.start()
    for s in range(parts):
        go(t_mate(0, s))
    for h in range(cuts):
        go(b_mate(0, h, True, core))

    aligned = piece % 16 == 0

    def t_split(start, size):
        rows = pl.ds(pl.multiple_of(start, 16), size)
        for k in range(tiles):
            high, low = split(t_all[pl.ds(start * tiles + k, size, stride=tiles), :])
            t_high[rows, k * lanes:(k + 1) * lanes] = high.astype(BF16)
            t_low[rows, k * lanes:(k + 1) * lanes] = low.astype(BF16)

    def t_part(owner, s):
        if aligned:
            t_split(owner * rows_t + s * piece, piece)

    def t_over(e, s):
        owner = chip_at(-e) * 2 + (1 - core)
        t_landed(owner, s, tm_send.at[e, s], tm_recv.at[e, s])
        t_part(owner, s)

    def relay(v):
        d, g = rounds[v - 1]
        for from_left in sorted((True, False), key=lambda side: sizes[cut_of(g, side)]):
            if carried(d, from_left):
                arrive(d, g, from_left)
                if d + 1 < reach or (d + 1 == reach and g == 0 and carried(reach, from_left)):
                    go(hop(d + 1, g, from_left))
                go(b_mate(d, cut_of(g, from_left), from_left, core))

    def b_over(v):
        if v == 0:
            for h in range(cuts):
                b_mate(0, h, True, 1 - core).wait_recv()
            return
        d, g = rounds[v - 1]
        for from_left in (True, False):
            if carried(d, from_left):
                b_mate(d, cut_of(g, from_left), from_left, 1 - core).wait_recv()

    def t_step(s):
        for e in range(1, chips):
            owner = chip_at(-e) * 2 + core
            t_landed(owner, s, tx_send.at[e - 1, s], tx_recv.at[e - 1, s])
            go(t_mate(e, s))
            t_part(owner, s)
        if s:
            for e in range(1, chips):
                t_over(e, s - 1)

    own_t.wait()
    if aligned:
        @pl.loop(0, parts)
        def _(s):
            t_part(aux, s)

        for s in range(parts):
            t_over(0, s)
    else:
        for s in range(parts):
            t_over(0, s)
    own_b.wait()

    def first_block(slot):
        return (chip_at(slot // q) * 2 + core) * q + lax.rem(slot, q)

    def reach_of(o):
        return (o, False) if o <= reach and o < n - o else (n - o, True)

    def about(table, slot, h):
        away = lax.rem(lookup(where, first_block(slot)) - spot + n, n)
        return lookup([table[reach_of(o) + (h,)] for o in range(n)], away)

    ready = [[about(due, slot, h) for h in range(cuts)] for slot in range(chips * q)]
    origin = [[about(place, slot, h) for h in range(cuts)] for slot in range(chips * q)]

    def pick(table, slot, h):
        return lookup([row[h] for row in table], slot)

    def extent(h):
        return (starts[h], sizes[h]) if h is not None else (0, rows_b)

    ahead = (2 * rows_t // lanes) if chips == 2 and aligned else 0
    near = pl.ds(pl.multiple_of(chip * (tiles - ahead) * lanes, lanes), ahead * lanes)
    rest_of = pl.ds(pl.multiple_of((1 - chip) * ahead * lanes, lanes), (tiles - ahead) * lanes)

    def g_sum(slot, h, span):
        count = extent(h)[1]
        cuts_in = range(cuts) if h is None else [h]
        pieces = []
        for level in range(2):
            parts_in = [
                b_all[level, pl.ds(pl.multiple_of(pick(origin, slot, c), 8), sizes[c]), span] for c in cuts_in
            ]
            pieces.append(split(jnp.concatenate(parts_in, axis=0) if len(parts_in) > 1 else parts_in[0]))
        high = jnp.concatenate([p[0] for p in pieces], axis=0)
        low = jnp.concatenate([p[1] for p in pieces], axis=0)
        both = jnp.concatenate([high, low], axis=0).astype(BF16)
        main = jnp.dot(both, t_high[span, :], preferred_element_type=F32)
        rest = jnp.dot(high.astype(BF16), t_low[span, :], preferred_element_type=F32)
        return main[:2 * count] + (main[2 * count:] + rest)

    def g_part(slot, h, begun_before=False):
        start, count = extent(h)
        if begun_before:
            total = g_ahead[slot] + g_sum(slot, h, rest_of)
        else:
            total = g_sum(slot, h, slice(None))
        high, low = split(total)
        for level in range(2):
            part = slice(level * count, (level + 1) * count)
            lane = slice(level * width, (level + 1) * width)
            g_high[slot, start:start + count, lane] = high[part].astype(BF16)
            g_low[slot, start:start + count, lane] = low[part].astype(BF16)

    def product(high, low, cols_high, cols_low):
        rows = high.shape[0]
        dot = functools.partial(lax.dot_general, dimension_numbers=NT, preferred_element_type=F32)
        if rows_b % 16 == 0:
            main = dot(jnp.concatenate([high, low], axis=0), cols_high)
            return main[:rows] + (main[rows:] + dot(high, cols_low))
        return dot(high, cols_high) + (dot(low, cols_high) + dot(high, cols_low))

    def columns(j, count):
        return [ref[pl.ds(j, count)].reshape(count * lanes, 2 * width) for ref in (b_high, b_low)]

    def p_cross(e, i, h, j):
        rows = pl.ds(pl.multiple_of(i * rows_b + starts[h], 8), sizes[h])
        return pltpu.make_async_remote_copy(
            src_ref=outbox.at[e - 1, j, rows], dst_ref=inbox.at[e - 1, j, rows],
            send_sem=px_send.at[e - 1, i, h, j], recv_sem=px_recv.at[e - 1, i, h, j],
            device_id=(pair, chip_at(e) * 2 + core), device_id_type=MESH,
        )

    def full(v):
        return filled[v] // lanes

    def older(v, j):
        @pl.loop(q, slots)
        def _(turn):
            slot = slot_of(turn - q)
            e, i = slot // q, lax.rem(slot, q)
            old = [pick(ready, slot, h) < v for h in range(cuts)]

            @pl.when(functools.reduce(jnp.logical_or, old))
            def _():
                rows = pl.ds(pl.multiple_of(i * rows_b, 8), rows_b)
                outbox[e - 1, j, rows] = product(g_high[slot], g_low[slot], *columns(j, 1))
                for h in range(cuts):
                    @pl.when(old[h])
                    def _(h=h):
                        p_cross(e, i, h, j).start()

    def block_ready(slot):
        return functools.reduce(jnp.maximum, [pick(ready, slot, h) for h in range(cuts)])

    slots = chips * q
    swaps = [jnp.where(block_ready(e * q + 1) < block_ready(e * q), 1, 0) if q == 2 else 0 for e in range(chips)]

    def slot_of(turn):
        if chips == 2 and q == 2:
            e = 1 - turn // 2
            return e * q + lax.rem(turn + lookup(swaps, e), 2)
        return lax.rem(turn + q, slots)

    def newer(h, count, wanted, low=0, high=slots, begun_before=False):
        start, size = extent(h)

        @pl.loop(low, high)
        def _(turn):
            slot = slot_of(turn)
            e, i = slot // q, lax.rem(slot, q)

            @pl.when(wanted(slot))
            def _():
                g_part(slot, h, begun_before)

                @pl.when(e > 0)
                def _():
                    rows = pl.ds(pl.multiple_of(i * rows_b + start, 8), size)
                    left = [ref[slot, start:start + size, :] for ref in (g_high, g_low)]

                    def some(j, k):
                        value = product(*left, *columns(j, k))
                        for t in range(k):
                            outbox[e - 1, j + t, rows] = value[:, t * lanes:(t + 1) * lanes]
                            for c in range(cuts) if h is None else [h]:
                                p_cross(e, i, c, j + t).start()

                    if count // 2:
                        @pl.loop(0, count // 2)
                        def _(k):
                            some(2 * k, 2)
                    if count % 2:
                        some(count - 1, 1)

    def tile_split(j):
        for level in range(2):
            high, low = split(b_all[level, pl.ds(j * lanes, lanes), :])
            b_high[j, :, level * width:(level + 1) * width] = high.astype(BF16)
            b_low[j, :, level * width:(level + 1) * width] = low.astype(BF16)

    def prepare(v):
        b_over(v)
        for j in range(full(v - 1) if v else 0, full(v)):
            tile_split(j)

    def begun(slot):
        return block_ready(slot) <= first

    assert all(v < first for (d, _, _), v in due.items() if v <= first) or not ahead
    def stage(wanted):
        if ahead:
            @pl.loop(0, slots)
            def _(turn):
                slot = slot_of(turn)

                @pl.when(wanted(slot))
                def _():
                    g_ahead[slot] = g_sum(slot, None, near)

    prepare(0)
    stage(lambda slot: block_ready(slot) == 0)
    step = 0
    for v in range(1, first + 1):
        upto = parts * (2 * v - 1) // (2 * first)
        for s in range(step, upto):
            t_step(s)
        step = upto
        relay(v)
        if v > 1:
            prepare(v - 1)
    stage(lambda slot: jnp.logical_and(begun(slot), block_ready(slot) > 0))
    prepare(first)
    if first + 1 < n_events:
        relay(first + 1)
    for s in range(step, parts):
        t_step(s)
    for e in range(1, chips):
        t_over(e, parts - 1)
    if not aligned:
        @pl.loop(0, width // 128)
        def _(i):
            t_split(i * 128, 128)

    def own_columns(j, count):
        if rows_b % 16 == 0:
            left = [ref[:q].reshape(q * rows_b, 2 * width) for ref in (g_high, g_low)]
            value = product(*left, *columns(j, count))
            for k in range(count):
                mine[j + k] = value[:, k * lanes:(k + 1) * lanes]
        else:
            for k in range(count):
                @pl.loop(0, q)
                def _(i):
                    mine[j + k, pl.ds(pl.multiple_of(i * rows_b, 8), rows_b)] = product(
                        g_high[i], g_low[i], *columns(j + k, 1))

    def own_pairs(low, high):
        @pl.loop(low, high)
        def _(k):
            own_columns(2 * k, 2)

    base = min(first + 1, n_events - 1)
    if base > first:
        prepare(base)

    def joined(slot):
        return block_ready(slot) == base

    late = block_ready(slot_of(slots - q - 1)) > base

    def group(low, high, when=True):
        newer(None, full(base), lambda slot: jnp.logical_and(begun(slot), when), low, high, bool(ahead))
        if base > first:
            newer(None, full(base), lambda slot: jnp.logical_and(joined(slot), when), low, high)

    some = (slots - q + 1) // 2
    most = slots - q + q // 2
    idle = block_ready(slot_of(0)) > base
    group(0, some)
    group(slots - q, slots, idle)
    if first + 2 < n_events:
        relay(first + 2)
    group(some, slots - q)
    group(slots - q, most, jnp.logical_not(idle))
    group(most, slots, jnp.logical_and(late, jnp.logical_not(idle)))
    for v in range(base + 1, n_events):
        if v > first + 2:
            relay(v)
        prepare(v)
        for j in range(full(v - 1), full(v)):
            older(v, j)
        if cuts == 1 or v == n_events - 1:
            newer(None, full(v), lambda slot: block_ready(slot) == v)
        else:
            for h in range(cuts):
                newer(h, full(v), lambda slot: pick(ready, slot, h) == v)

    group(most, slots, jnp.logical_not(jnp.logical_or(idle, late)))
    own_pairs(0, tiles // 2)
    if tiles % 2:
        own_columns(tiles - 1, 1)

    def block_of(d, from_left):
        return at(-d if from_left else d)

    segments = [[] for _ in range(tiles)]
    seen = set()
    for (d, from_left, h), begin in sorted(place.items(), key=lambda item: item[1]):
        if begin in seen:
            continue
        seen.add(begin)
        for j in range(begin // lanes, (begin + sizes[h] - 1) // lanes + 1):
            low, high = max(begin, j * lanes), min(begin + sizes[h], (j + 1) * lanes)
            segments[j].append((low - j * lanes, high - low, d, from_left, starts[h] + low - begin))

    lane = lax.broadcasted_iota(jnp.int32, (1, lanes), 1)

    for j in range(tiles):
        for e in range(1, chips):
            for i in range(q):
                for h in range(cuts):
                    p_cross(e, i, h, j).wait_recv()
        total = mine[j]
        for e in range(1, chips):
            total = total + inbox[e - 1, j]
        for begin, size, d, from_left, offset in segments[j]:
            goal = block_of(d, from_left) * rows_b + offset
            turned = pltpu.roll(total, lax.rem(goal - begin + lanes, lanes), 1)
            for part in range(2):
                into = goal // lanes + part
                inside = jnp.logical_and(lane >= goal - into * lanes, lane < goal - into * lanes + size)

                @pl.when(goal + size > into * lanes)
                def _():
                    at_rows = pl.ds(into, rows_t, stride=tiles)
                    final[at_rows, :] = jnp.where(inside, turned, final[at_rows, :])

    done = pltpu.make_async_copy(final, out, out_sem.at[0])
    done.start()
    for copy in started:
        copy.wait_send()
    for e in range(1, chips):
        for i in range(q):
            for h in range(cuts):
                for j in range(tiles):
                    p_cross(e, i, h, j).wait_send()
    done.wait()


def per_device(n, n_aux, amplitudes, fitting):
    rows_t, pair_dev, width = amplitudes.shape
    count_fit, rows_b, _ = fitting.shape
    assert pair_dev == 1 and count_fit == 1 and rows_t % rows_b == 0
    chips = n_aux // 2
    parts = max([p for p in range(1, PARTS + 1) if rows_t % (16 * p) == 0], default=1)
    cuts = CUTS if rows_b % 16 == 0 and n > 2 else 1
    reach = n // 2
    lanes = 128
    tiles = width // lanes
    q = rows_t // rows_b
    dma = pltpu.SemaphoreType.DMA
    half = pltpu.VMEM((width, width), BF16)
    tiled = pltpu.VMEM((tiles, lanes, 2 * width), BF16)
    block = pltpu.VMEM((chips * q, rows_b, 2 * width), BF16)
    out = pl.pallas_call(
        functools.partial(kernel, n, chips, parts, cuts),
        out_shape=jax.ShapeDtypeStruct((rows_t * tiles, lanes), F32),
        in_specs=[pl.BlockSpec(memory_space=pltpu.HBM)] * 2,
        out_specs=pl.BlockSpec(memory_space=pl.ANY),
        scratch_shapes=[
            pltpu.VMEM((width * tiles, lanes), F32), half, half,
            pltpu.VMEM((2, width, width), F32), tiled, tiled, block, block,
            pltpu.VMEM((chips - 1, tiles, q * rows_b, lanes), F32),
            pltpu.VMEM((chips - 1, tiles, q * rows_b, lanes), F32),
            pltpu.VMEM((tiles, q * rows_b, lanes), F32), pltpu.VMEM((rows_t * tiles, lanes), F32),
            pltpu.VMEM((chips * q, 2 * rows_b, width), F32),
            dma((2,)), dma((1,)),
            dma((reach, cuts)), dma((reach, cuts)), dma((reach, cuts)), dma((reach, cuts)),
            dma((reach + 1, 2, cuts)), dma((reach + 1, 2, cuts)),
            dma((chips - 1, parts)), dma((chips - 1, parts)),
            dma((chips, parts)), dma((chips, parts)),
            dma((chips - 1, q, cuts, tiles)), dma((chips - 1, q, cuts, tiles)),
        ],
        compiler_params=pltpu.CompilerParams(
            collective_id=0, has_side_effects=True, vmem_limit_bytes=105 << 19
        ),
    )(*[pltpu.with_memory_space_constraint(v, pltpu.HBM) for v in (
        amplitudes.reshape(rows_t * tiles, lanes), fitting.reshape(rows_b, width))])
    return out.reshape(rows_t, pair_dev, width)


def solution(mesh):
    spec = P("aux", "pair", None)
    return jax.shard_map(
        functools.partial(per_device, mesh.shape["pair"], mesh.shape["aux"]),
        mesh=mesh, in_specs=(spec, spec), out_specs=spec, check_vma=False,
    )
```
